32 devices in a mesh: wide: 2 (over x), narrow: 4 (over y, core), seq: 4 (over z).
Axes of the slice: x: 2, y: 2, z: 4, core: 2. Of those that a mesh axis runs over, the one named last changes fastest.
Arguments:
- attn_query: bfloat16 [1024, 73728], P(('seq', 'wide'), 'narrow'), parts along dimension 0, may hold values from -6 to 6
- key_latent: bfloat16 [1024, 576], P(('seq', 'wide')), parts along dimension 0, may hold values from -6 to 6
- lse_attn: float32 [128, 1024], P('narrow', ('seq', 'wide')), parts along dimension 1, may hold values from 1 to 3
- index_query: bfloat16 [1024, 8192], P(('seq', 'wide'), 'narrow'), parts along dimension 0, may hold values from -6 to 6
- index_key: bfloat16 [1024, 128], P(('seq', 'wide')), parts along dimension 0, may hold values from -6 to 6
- index_weight: float32 [64, 1024], P('narrow', ('seq', 'wide')), parts along dimension 1, may hold values from -0.75 to 0.75
- lse_index: float32 [1024], P(('seq', 'wide')), parts along dimension 0, may hold values from 0 to 1
- block_order: int32 [8], P('seq'), parts along dimension 0, may hold values from 0 to 127, as said below
Outputs:
- d_index_query: float32 [1024, 8192], P(('seq', 'wide'), 'narrow'), parts along dimension 0
- d_index_weight: float32 [64, 1024], P('narrow', ('seq', 'wide')), parts along dimension 1
- d_index_key: float32 [1024, 128], P(('seq', 'wide')), parts along dimension 0
The draws below stay inside these ranges and needn't reach their ends.
There are 4 independent parts, one for each index of `seq`. The reference program is written for one: setup_inputs(seed, part) draws one part's arguments, and reference() takes and returns one part's arrays. A program takes and returns all parts, laid end to end along the dimension named above; each array names one. Nothing has to cross between parts.
Inputs may be any that keep to these rules, and one draw needn't show every extreme that they name: Index d of wide holds tokens 128 * block_order[d] to 128 * block_order[d] + 127 of the context; the values are distinct.
All inputs are finite; a program needn't handle non-finite values.
Results may differ from the reference program's by a relative error of at most 0.008.
Values may be sent and summed in bfloat16 or wider, within the bound.
No kernel may reach another device: no remote copies, remote signals or barrier semaphores. Data moves between devices by JAX's collectives and lax.ppermute only.
A program may use at most 64 MiB of HBM per device.

```python
import jax
import jax.numpy as jnp
from jax import lax

HEADS = 128
KV_RANK = 512
ROPE = 64
IHEADS = 64
IDIM = 128
TOK_DEV = 128
KEY_WIDTH = 576
TOKENS = 256
N_WIDE = 2


def draw_block_order(key, part):
    first_key, second_key = jax.random.split(jax.random.fold_in(key, 7331))
    span = 64 * N_WIDE
    chosen = jax.random.permutation(first_key, span - 1)[:N_WIDE - 1].astype(jnp.int32)
    values = jnp.concatenate([chosen, jnp.full((1,), span - 1, jnp.int32)])
    return jax.random.permutation(second_key, values).astype(jnp.int32)


def shard_levels(stream_key, shape, cuts, least, top_value):
    def one(axis_at, blocks):
        draws = jax.random.uniform(jax.random.fold_in(jax.random.fold_in(stream_key, 6), axis_at), (blocks,), jnp.float32, least / len(cuts), top_value / len(cuts))
        return jnp.repeat(jnp.exp(draws), shape[axis_at] // blocks).reshape((-1,) + (1,) * (len(shape) - axis_at - 1))

    loudness = one(*cuts[0])
    for cut in cuts[1:]:
        loudness = loudness * one(*cut)
    return loudness


def centred(key, extent, spread, most, pieces=(), held_as=jnp.bfloat16):
    drawn = jax.random.normal(key, extent, jnp.float32) * spread
    if len(pieces) > 0:
        drawn = shard_levels(key, extent, pieces, -0.22, 0.18) * drawn
    return jnp.clip(drawn, min=-most, max=most).astype(held_as)


def setup_inputs(seed: int = 0, part: int = 0) -> dict:
    seeds = jax.random.split(jax.random.key(seed), 9)
    part_keys = jax.random.split(jax.random.fold_in(seeds[8], part), 9)
    return {
        "attn_query": centred(part_keys[0], (TOKENS, HEADS * KEY_WIDTH), 1.0, 6.0, ((0, 2), (1, 4))),
        "key_latent": centred(part_keys[1], (TOKENS, KEY_WIDTH), 1.0, 6.0, ((0, 2),)),
        "lse_attn": jnp.clip(1.0 + 2.0 * jax.random.uniform(part_keys[2], (HEADS, TOKENS), jnp.float32) ** shard_levels(part_keys[2], (HEADS, TOKENS), ((0, 4), (1, 2)), -0.2, 0.2), 1.0, 3.0),
        "index_query": centred(part_keys[3], (TOKENS, IHEADS * IDIM), 1.0, 6.0, ((0, 2), (1, 4))),
        "index_key": centred(part_keys[4], (TOKENS, IDIM), 1.0, 6.0, ((0, 2),)),
        "index_weight": centred(part_keys[5], (IHEADS, TOKENS), IHEADS ** -0.5, 0.75, ((0, 4), (1, 2)), jnp.float32),
        "lse_index": jnp.clip(1.0 * jax.random.uniform(part_keys[6], (TOKENS,), jnp.float32) ** shard_levels(part_keys[6], (TOKENS,), ((0, 2),), -0.2, 0.2), 0.0, 1.0),
        "block_order": draw_block_order(jax.random.fold_in(jax.random.fold_in(seeds[8], part), 71), part),
    }


attn_scale = 192.0 ** -0.5


def reference(attn_query, key_latent, lse_attn, index_query, index_key, index_weight, lse_index, block_order):
    key_width = KV_RANK + ROPE
    query_heads = attn_query.reshape(TOKENS, HEADS, key_width)
    index_heads = index_query.reshape(TOKENS, IHEADS, IDIM)
    offsets = jnp.arange(TOKENS, dtype=jnp.int32)
    position = block_order[offsets // TOK_DEV].astype(jnp.int32) * TOK_DEV + offsets % TOK_DEV
    keys_full = key_latent.astype(jnp.float32)
    ikeys_full = index_key.astype(jnp.float32)
    index_scale = IDIM ** -0.5

    def one_block(key_total, block_index):
        start = (block_index * TOK_DEV).astype(jnp.int32)
        queries = lax.dynamic_slice_in_dim(query_heads, start, TOK_DEV, 0).astype(jnp.float32)
        iqueries = lax.dynamic_slice_in_dim(index_heads, start, TOK_DEV, 0).astype(jnp.float32)
        lse_rows = jnp.transpose(lax.dynamic_slice_in_dim(lse_attn, start, TOK_DEV, 1))
        weight_rows = jnp.transpose(lax.dynamic_slice_in_dim(index_weight, start, TOK_DEV, 1))
        lse_share = lax.dynamic_slice_in_dim(lse_index, start, TOK_DEV, 0)
        query_pos = lax.dynamic_slice_in_dim(position, start, TOK_DEV, 0)
        causal = query_pos[:, None] >= position[None, :]
        scores = jnp.einsum("thc,sc->ths", queries, keys_full) * attn_scale
        target = jnp.sum(jnp.exp(scores - lse_rows[:, :, None]), axis=1) / HEADS
        logits = jnp.einsum("tjc,sc->tjs", iqueries, ikeys_full) * index_scale
        active = jnp.maximum(logits, 0.0)
        score = jnp.einsum("tjs,tj->ts", active, weight_rows)
        difference = jnp.where(causal, jnp.exp(score - lse_share[:, None]) - target, 0.0)
        grad_weight = jnp.einsum("ts,tjs->jt", difference, active)
        coefficient = (difference[:, None, :] * weight_rows[:, :, None] * (logits > 0.0).astype(jnp.float32) * index_scale).astype(jnp.bfloat16)
        coef_full = coefficient.astype(jnp.float32)
        grad_query = jnp.einsum("tjs,sc->tjc", coef_full, ikeys_full)
        grad_key = jnp.einsum("tjs,tjc->sc", coef_full, iqueries)
        return key_total + grad_key, (grad_query, grad_weight)

    start_total = jnp.zeros((TOKENS, IDIM), jnp.float32)
    key_total, stacked = lax.scan(one_block, start_total, jnp.arange(N_WIDE, dtype=jnp.int32))
    grad_query, grad_weight = stacked
    d_index_query = grad_query.reshape(TOKENS, IHEADS * IDIM)
    d_index_weight = jnp.transpose(grad_weight, (1, 0, 2)).reshape(IHEADS, TOKENS)
    return d_index_query, d_index_weight, key_total
```

```python
import functools

import jax
import jax.numpy as jnp
from jax import lax
from jax.experimental import pallas as pl
from jax.experimental.pallas import tpu as pltpu
from jax.sharding import PartitionSpec as P


HEADS = 128
attn_scale = 192.0 ** (-0.5)
F32 = jnp.float32
BF16 = jnp.bfloat16


def each(count, step):
    if count <= 2:
        for i in range(count):
            step(i)
    else:
        lax.fori_loop(0, count, lambda i, _: (step(i), None)[1], None)


def vmem():
    return pl.BlockSpec(memory_space=pltpu.VMEM)


def smem():
    return pl.BlockSpec(memory_space=pltpu.SMEM)


def call(kernel, out_shape, in_specs, scratch=(), limit=8 << 20, flops=0, moved=0):
    return pl.pallas_call(
        kernel,
        out_shape=out_shape,
        in_specs=in_specs,
        out_specs=jax.tree.map(lambda _: vmem(), out_shape),
        scratch_shapes=list(scratch),
        cost_estimate=pl.CostEstimate(flops=flops, bytes_accessed=moved, transcendentals=0),
        compiler_params=pltpu.CompilerParams(vmem_limit_bytes=limit),
    )


def block_sums(query, keys_ref, lse_ref, iquery_ref, ikey_ref, weight_ref, part_ref, active_ref, pair_ref):
    index_width = ikey_ref.shape[1]
    iheads = iquery_ref.shape[1] // index_width
    keys, tokens = part_ref.shape[1:]
    index_scale = index_width ** (-0.5)
    score = jnp.zeros((keys, tokens), F32)
    for j in range(iheads):
        logits = lax.dot_general(
            ikey_ref[...],
            iquery_ref[:, j * index_width : (j + 1) * index_width],
            (((1,), (1,)), ((), ())),
            preferred_element_type=F32,
        )
        active = jnp.maximum(logits * index_scale, 0.0)
        active_ref[:, j * tokens : (j + 1) * tokens] = active
        score = score + active * weight_ref[j : j + 1, :]
    part_ref[1] = score

    width = keys_ref.shape[0]
    pair_ref[...] = jnp.zeros_like(pair_ref)
    pair_ref[:width, :keys] = keys_ref[...]
    pair_ref[width:, keys:] = keys_ref[...]
    lse_columns = jnp.transpose(lse_ref[...])
    total = jnp.zeros((tokens, keys), F32)
    for p in range(lse_ref.shape[0] // 2):
        both = jnp.dot(query(p), pair_ref[...], preferred_element_type=F32)
        for side in range(2):
            h = 2 * p + side
            scores = both[:, side * keys : (side + 1) * keys] * attn_scale
            total = total + jnp.exp(scores - lse_columns[:, h : h + 1])
    part_ref[0] = jnp.transpose(total) * (1.0 / HEADS)


def own_kernel(
    query_hbm, keys_hbm, lse_hbm, iquery_hbm, ikey_hbm, weight_hbm,
    part_ref, active_ref, query_ref, lse_ref, iquery_ref, ikey_ref, weight_ref,
    pair_ref, keys_ref, sems,
):
    width = keys_ref.shape[0]
    pairs = query_ref.shape[1] // (2 * width)
    moves = [
        pltpu.make_async_copy(src, dst, sems.at[i])
        for i, (src, dst) in enumerate(
            (
                (ikey_hbm, ikey_ref),
                (iquery_hbm, iquery_ref),
                (weight_hbm, weight_ref),
                (lse_hbm, lse_ref),
                (keys_hbm, keys_ref),
            )
        )
    ]
    chunks = sems.shape[0] - len(moves)
    span = pairs // chunks * 2 * width
    moves += [
        pltpu.make_async_copy(
            query_hbm.at[:, i * span : (i + 1) * span],
            query_ref.at[:, i * span : (i + 1) * span],
            sems.at[len(moves) + i],
        )
        for i in range(chunks)
    ]
    for move in moves:
        move.start()
    for move in moves[:5]:
        move.wait()

    def query(p):
        if p % (pairs // chunks) == 0:
            moves[5 + p // (pairs // chunks)].wait()
        return query_ref[:, 2 * p * width : 2 * (p + 1) * width]

    block_sums(
        query, keys_ref, lse_ref, iquery_ref, ikey_ref, weight_ref, part_ref, active_ref, pair_ref
    )


def other_kernel(query_ref, keys_ref, lse_ref, iquery_ref, ikey_ref, weight_ref, part_ref, active_ref, pair_ref):
    width = keys_ref.shape[0]

    def query(p):
        return query_ref[:, 2 * p * width : 2 * (p + 1) * width]

    block_sums(
        query, keys_ref, lse_ref, iquery_ref, ikey_ref, weight_ref, part_ref, active_ref, pair_ref
    )


def key_grad_kernel(
    blocks, order_ref, chip_ref, recv_ref, lse_ref, active_ref, weight_ref, iquery_ref,
    grad_ref, coef_ref, diff_ref,
):
    keys, tokens = chip_ref.shape[2:]
    index_width = grad_ref.shape[2]
    iheads = weight_ref.shape[0]
    index_scale = index_width ** (-0.5)
    place = lax.axis_index("wide")

    def block(b):
        source = lax.rem(place - b + blocks, blocks)
        target = chip_ref[b, 0] + recv_ref[b, 0].astype(F32)
        score = chip_ref[b, 1] + recv_ref[b, 1].astype(F32)
        key_at = lax.broadcasted_iota(jnp.int32, (keys, tokens), 0)
        query_at = lax.broadcasted_iota(jnp.int32, (keys, tokens), 1)
        causal = (order_ref[place] - order_ref[source]) * tokens + query_at >= key_at
        difference = jnp.where(causal, jnp.exp(score - lse_ref[...]) - target, 0.0)
        diff_ref[b] = difference
        for j in range(iheads):
            scaled = difference * (weight_ref[j : j + 1, :] * index_scale)
            coef = jnp.where(active_ref[b, :, j * tokens : (j + 1) * tokens] > 0.0, scaled, 0.0)
            coef_ref[b, :, j * tokens : (j + 1) * tokens] = coef.astype(BF16)
        total = jnp.zeros((keys, index_width), F32)
        for p in range(iheads // 2):
            rows = jnp.concatenate(
                [
                    iquery_ref[:, (2 * p + i) * index_width : (2 * p + i + 1) * index_width]
                    for i in range(2)
                ],
                axis=0,
            )
            total = total + jnp.dot(
                coef_ref[b, :, 2 * p * tokens : 2 * (p + 1) * tokens],
                rows,
                preferred_element_type=F32,
            )
        grad_ref[b] = total

    each(blocks, block)


def query_grad_kernel(blocks, coef_ref, diff_ref, active_ref, ikey_ref, grad_ref, weight_grad_ref):
    _, tokens = diff_ref.shape[1:]
    index_width = ikey_ref.shape[2]
    iheads = weight_grad_ref.shape[0]
    grad_ref[...] = jnp.zeros_like(grad_ref)
    weight_grad_ref[...] = jnp.zeros_like(weight_grad_ref)

    def block(b):
        for j in range(iheads):
            at = slice(j * tokens, (j + 1) * tokens)
            grad_ref[:, j * index_width : (j + 1) * index_width] += lax.dot_general(
                coef_ref[b, :, at], ikey_ref[b], (((0,), (0,)), ((), ())), preferred_element_type=F32
            )
            weight_grad_ref[j : j + 1, :] += jnp.sum(
                diff_ref[b] * active_ref[b, :, at], axis=0, keepdims=True
            )

    each(blocks, block)


def body(
    attn_query, key_latent, lse_attn, index_query, index_key, index_weight, lse_index, block_order
):
    tokens, key_width = key_latent.shape
    index_width = index_key.shape[1]
    heads = attn_query.shape[1] // key_width
    iheads = index_query.shape[1] // index_width
    wide, narrow = lax.axis_size("wide"), lax.axis_size("narrow")
    ranks = range(wide * narrow)

    def send(block, step, flip):
        route = [(r, (r // narrow - step) % wide * narrow + (r % narrow ^ flip)) for r in ranks]
        return lax.ppermute(block, ("wide", "narrow"), route)

    own_keys = jnp.transpose(key_latent)
    keys, ikeys = [own_keys], [index_key]
    for b in range(1, wide):
        keys.append(send(own_keys, -b, 0))
        ikeys.append(send(index_key, -b, 0))

    like = jax.ShapeDtypeStruct
    part = like((2, tokens, tokens), F32)
    act = like((tokens, iheads * tokens), F32)
    pair_shape = pltpu.VMEM((2 * key_width, 2 * tokens), BF16)
    work = dict(
        flops=2 * tokens * tokens * (heads * key_width + iheads * index_width),
        moved=attn_query.size * 2,
    )
    inputs = (attn_query, own_keys, lse_attn, index_query, index_key, index_weight)
    chunks = 4 if heads % 8 == 0 else 1
    own = call(
        own_kernel,
        (part, act)
        + tuple(like(a.shape, a.dtype) for a in (attn_query, lse_attn, index_query, index_key, index_weight)),
        [pl.BlockSpec(memory_space=pltpu.MemorySpace.HBM)] * 6,
        [pair_shape, pltpu.VMEM(own_keys.shape, BF16), pltpu.SemaphoreType.DMA((5 + chunks,))],
        limit=14 << 20,
        **work,
    )(*(pltpu.with_memory_space_constraint(x, pltpu.MemorySpace.HBM) for x in inputs))
    query, lse, iquery, ikey, weight = own[2:]
    other = call(other_kernel, (part, act), [vmem()] * 6, [pair_shape], limit=14 << 20, **work)
    found = [own[:2]] + [
        other(query, k, lse, iquery, ik, weight) for k, ik in zip(keys[1:], ikeys[1:])
    ]
    ikeys[0] = ikey
    active = jnp.stack([a for _, a in found])
    chip = jnp.stack([p + send(p, 0, 1) for p, _ in found])
    recv = send(chip.astype(BF16), 0, 2)

    grad, coef, difference = call(
        functools.partial(key_grad_kernel, wide),
        (
            jax.ShapeDtypeStruct((wide, tokens, index_width), F32),
            jax.ShapeDtypeStruct((wide, tokens, iheads * tokens), BF16),
            jax.ShapeDtypeStruct((wide, tokens, tokens), F32),
        ),
        [smem()] + [vmem()] * 6,
        limit=16 << 20,
        flops=2 * wide * tokens * tokens * iheads * index_width,
        moved=wide * tokens * tokens * iheads * 6,
    )(block_order, chip, recv, lse_index[None, :], active, weight, iquery)

    grad_query, grad_weight = call(
        functools.partial(query_grad_kernel, wide),
        (
            jax.ShapeDtypeStruct((tokens, iheads * index_width), F32),
            jax.ShapeDtypeStruct((iheads, tokens), F32),
        ),
        [vmem()] * 4,
        limit=16 << 20,
        flops=2 * wide * tokens * tokens * iheads * index_width,
        moved=wide * tokens * tokens * iheads * 6,
    )(coef, difference, active, jnp.stack(ikeys))

    pair = (grad + send(grad, 0, 1)).astype(BF16)
    key_grad = jnp.zeros((tokens, index_width), F32)
    for b in range(wide):
        near = send(pair[b], b, 0) if b else pair[b]
        far = send(pair[b], b, 2)
        key_grad = key_grad + (near.astype(F32) + far.astype(F32))
    return grad_query, grad_weight, key_grad


def solution(mesh):
    in_specs = (
        P(("seq", "wide"), "narrow"),
        P(("seq", "wide"), None),
        P("narrow", ("seq", "wide")),
        P(("seq", "wide"), "narrow"),
        P(("seq", "wide"), None),
        P("narrow", ("seq", "wide")),
        P(("seq", "wide")),
        P("seq"),
    )
    out_specs = (
        P(("seq", "wide"), "narrow"),
        P("narrow", ("seq", "wide")),
        P(("seq", "wide"), None),
    )
    return jax.shard_map(
        body,
        mesh=mesh,
        in_specs=in_specs,
        out_specs=out_specs,
        check_vma=False,
    )
```

```python
import functools
import math

import jax
import jax.numpy as jnp
from jax import lax
from jax.experimental import pallas as pl
from jax.experimental.pallas import tpu as pltpu
from jax.sharding import PartitionSpec as P


HEADS = 128
SPAN = 8
CHUNKS = 2
attn_scale = 192.0 ** (-0.5)
F32 = jnp.float32
BF16 = jnp.bfloat16


def vmem():
    return pl.BlockSpec(memory_space=pltpu.VMEM)


def call(kernel, out_shape, in_specs, scratch=(), limit=8 << 20, flops=0, moved=0):
    return pl.pallas_call(
        kernel,
        out_shape=out_shape,
        in_specs=in_specs,
        out_specs=jax.tree.map(lambda _: vmem(), out_shape),
        scratch_shapes=list(scratch),
        cost_estimate=pl.CostEstimate(flops=flops, bytes_accessed=moved, transcendentals=0),
        compiler_params=pltpu.CompilerParams(vmem_limit_bytes=limit),
    )


def side_by_side(refs):
    return jnp.concatenate([ref[...] for ref in refs], axis=1)


def block_sums(turned, packed, lse_ref, iturned_ref, weight_ref, part_ref, active_ref):
    tokens = part_ref.shape[2]
    heads, iheads = lse_ref.shape[0], weight_ref.shape[0]
    index_width = iturned_ref.shape[0] // iheads
    index_scale = index_width ** (-0.5)
    width = packed.shape[0] - index_width
    late = -width % 128
    fill = jnp.zeros((late, packed.shape[1]), BF16)
    sides = [
        jnp.transpose(jnp.concatenate(parts, axis=0)) if late else jnp.transpose(packed[:width])
        for parts in ((packed[:width], fill), (fill, packed[:width]))
    ]
    score = 0.0
    for j in range(0, iheads, 2):
        rows = [iturned_ref.at[i * index_width : (i + 1) * index_width] for i in (j, j + 1)]
        logits = jnp.dot(packed[width:], side_by_side(rows), preferred_element_type=F32)
        active = jnp.maximum(logits * index_scale, 0.0)
        active_ref[:, j * tokens : (j + 2) * tokens] = active
        for i in range(2):
            score = score + active[:, i * tokens : (i + 1) * tokens] * weight_ref[j + i : j + i + 1, :]
    part_ref[1] = score

    total = 0.0
    for p in range(0, heads // 2, 2):
        pairs = [turned(p), turned(p + 1)]
        for side, keys in enumerate(sides):
            first = side * (width - late)
            rows = [pair.at[first : first + width + late] for pair in pairs]
            both = jnp.dot(keys, side_by_side(rows), preferred_element_type=F32) * attn_scale
            for i in range(2):
                h = 2 * (p + i) + side
                total = total + jnp.exp(both[:, i * tokens : (i + 1) * tokens] - lse_ref[h : h + 1, :])
    part_ref[0] = total * (1.0 / HEADS)


def load_kernel(order_hbm, *refs):
    count = (len(refs) - 3) // 2
    sources, held = refs[:count], refs[count : 2 * count - 1]
    mine_ref, live_ref, order_ref, sems = refs[2 * count - 1 :]
    packed_ref = held[0]
    width = sources[0].shape[0]
    held = (packed_ref.at[:width], packed_ref.at[width:], *held[1:])
    moves = [
        pltpu.make_async_copy(src, dst, sems.at[i])
        for i, (src, dst) in enumerate(zip((order_hbm, *sources), (order_ref, *held)))
    ]
    for move in moves:
        move.start()
    for move in moves:
        move.wait()
    half = mine_ref.shape[0]
    core = lax.axis_index("narrow") % 2
    mine_ref[...] = packed_ref[pl.ds(pl.multiple_of(core * half, half), half)]

    place, blocks = lax.axis_index("wide"), live_ref.shape[0]
    for b in range(blocks):
        source = lax.rem(place - b + blocks, blocks)
        live = (order_ref[place] > order_ref[source]).astype(F32)
        live_ref[b] = jnp.full(live_ref.shape[1:], live, F32)


def own_kernel(
    query_hbm, packed_ref, iquery_ref, lse_ref, weight_ref,
    part_ref, active_ref, turned_ref, iturned_ref, query_ref, sems,
):
    pair_width = query_ref.shape[1] // lse_ref.shape[0] * 2
    step = query_ref.shape[1] // sems.shape[0]
    moves = []
    for i in range(sems.shape[0]):
        at = slice(i * step, (i + 1) * step)
        moves.append(pltpu.make_async_copy(query_hbm.at[:, at], query_ref.at[:, at], sems.at[i]))
        moves[-1].start()

    def turned(p):
        at = p * pair_width
        if at % step == 0:
            moves[at // step].wait()
        at = slice(at, at + pair_width)
        turned_ref[at] = jnp.transpose(query_ref[:, at])
        return turned_ref.at[at]

    @pl.when(lax.axis_index("wide") >= 0)
    def _():
        index_width = iquery_ref.shape[1] // weight_ref.shape[0]
        for j in range(weight_ref.shape[0]):
            at = slice(j * index_width, (j + 1) * index_width)
            iturned_ref[at] = jnp.transpose(iquery_ref[:, at])
        block_sums(turned, packed_ref, lse_ref, iturned_ref, weight_ref, part_ref, active_ref)


def other_kernel(
    turned_ref, mine_ref, theirs_ref, lse_ref, iturned_ref, weight_ref,
    part_ref, active_ref, ikey_ref, packed_ref,
):
    pair_width = turned_ref.shape[0] // lse_ref.shape[0] * 2
    half = mine_ref.shape[0]
    core = lax.axis_index("narrow") % 2
    packed_ref[pl.ds(pl.multiple_of(core * half, half), half)] = mine_ref[...]
    packed_ref[pl.ds(pl.multiple_of((1 - core) * half, half), half)] = theirs_ref[...]
    ikey_ref[...] = packed_ref[packed_ref.shape[0] - ikey_ref.shape[0] :]

    def turned(p):
        return turned_ref.at[p * pair_width : (p + 1) * pair_width]

    block_sums(turned, packed_ref, lse_ref, iturned_ref, weight_ref, part_ref, active_ref)


def key_grad_kernel(
    step, live_ref, mine_ref, theirs_ref, lse_ref, active_ref, weight_ref, iquery_ref,
    grad_ref, coef_ref, diff_ref,
):
    keys, tokens = mine_ref.shape[1:]
    index_width = grad_ref.shape[1]
    iheads = weight_ref.shape[0]
    index_scale = index_width ** (-0.5)
    target = mine_ref[0] + theirs_ref[0]
    score = mine_ref[1] + theirs_ref[1]
    if step == 0:
        key_at = lax.broadcasted_iota(jnp.int32, (keys, tokens), 0)
        query_at = lax.broadcasted_iota(jnp.int32, (keys, tokens), 1)
        causal = query_at >= key_at
    else:
        causal = jnp.broadcast_to(live_ref[step], (keys, tokens)) > 0.0
    difference = jnp.where(causal, jnp.exp(score - lse_ref[...]) - target, 0.0)
    diff_ref[...] = difference
    total = jnp.zeros((keys, index_width), F32)
    span = math.gcd(iheads, SPAN)
    for first in range(0, iheads, span):
        for j in range(first, first + span):
            scaled = difference * (weight_ref[j : j + 1, :] * index_scale)
            coef = jnp.where(active_ref[:, j * tokens : (j + 1) * tokens] > 0.0, scaled, 0.0)
            coef_ref[:, j * tokens : (j + 1) * tokens] = coef.astype(BF16)
        rows = [
            iquery_ref[:, j * index_width : (j + 1) * index_width]
            for j in range(first, first + span)
        ]
        total = total + jnp.dot(
            coef_ref[:, first * tokens : (first + span) * tokens],
            jnp.concatenate(rows, axis=0),
            preferred_element_type=F32,
        )
    grad_ref[...] = total


def query_grad_kernel(blocks, *refs):
    coefs, diffs, actives, ikeys = (refs[i * blocks : (i + 1) * blocks] for i in range(4))
    grad_ref, weight_grad_ref = refs[4 * blocks :]
    tokens = diffs[0].shape[1]
    index_width = ikeys[0].shape[1]
    for j in range(weight_grad_ref.shape[0]):
        at = slice(j * tokens, (j + 1) * tokens)
        grad, weight_grad = 0.0, 0.0
        for coef, diff, active, ikey in zip(coefs, diffs, actives, ikeys):
            grad = grad + lax.dot_general(
                coef[:, at], ikey[...], (((0,), (0,)), ((), ())), preferred_element_type=F32
            )
            weight_grad = weight_grad + jnp.sum(diff[...] * active[:, at], axis=0, keepdims=True)
        grad_ref[:, j * index_width : (j + 1) * index_width] = grad
        weight_grad_ref[j : j + 1, :] = weight_grad


def body(
    attn_query, key_latent, lse_attn, index_query, index_key, index_weight, lse_index, block_order
):
    tokens, key_width = key_latent.shape
    index_width = index_key.shape[1]
    heads = attn_query.shape[1] // key_width
    iheads = index_query.shape[1] // index_width
    wide, narrow = lax.axis_size("wide"), lax.axis_size("narrow")
    ranks = range(wide * narrow)

    def send(block, step, flip, spread=False):
        route = []
        for r in ranks:
            turn = r % 2 * 2 if spread else flip
            route.append((r, (r // narrow - step) % wide * narrow + (r % narrow ^ turn)))
        return lax.ppermute(block, ("wide", "narrow"), route)

    like = jax.ShapeDtypeStruct
    hbm = pltpu.MemorySpace.HBM
    small = (
        jnp.transpose(key_latent),
        index_key,
        index_query,
        lse_attn,
        index_weight,
        lse_index[None, :],
    )
    half = (key_width + tokens) // 2
    packed, *small, mine, live = call(
        load_kernel,
        (like((key_width + tokens, tokens), BF16),)
        + tuple(like(a.shape, a.dtype) for a in small[2:])
        + (like((half, tokens), BF16), like((wide, 1, tokens), F32)),
        [pl.BlockSpec(memory_space=hbm)] * 7,
        [pltpu.SMEM(block_order.shape, jnp.int32), pltpu.SemaphoreType.DMA((7,))],
        limit=4 << 20,
    )(*(pltpu.with_memory_space_constraint(x, hbm) for x in (block_order, *small)))
    iquery, lse, weight, lse_row = small
    blocks = [None]
    for b in range(1, wide):
        first = send(mine, -b, 0)
        blocks.append((first, send(first, 0, 1)))

    part = like((2, tokens, tokens), F32)
    act = like((tokens, iheads * tokens), F32)
    work = dict(
        flops=2 * tokens * tokens * (heads * key_width + iheads * index_width),
        moved=attn_query.size * 2,
    )
    *own, turned, iturned = call(
        own_kernel,
        (
            part,
            act,
            like((heads * key_width, tokens), BF16),
            like((iheads * index_width, tokens), BF16),
        ),
        [pl.BlockSpec(memory_space=hbm)] + [vmem()] * 4,
        [
            pltpu.VMEM(attn_query.shape, BF16),
            pltpu.SemaphoreType.DMA((math.gcd(heads // 4, CHUNKS),)),
        ],
        limit=14 << 20,
        **work,
    )(pltpu.with_memory_space_constraint(attn_query, hbm), packed, iquery, lse, weight)
    other = call(
        other_kernel,
        (part, act, like(index_key.shape, BF16)),
        [vmem()] * 6,
        [pltpu.VMEM(packed.shape, BF16)],
        limit=10 << 20,
        **work,
    )
    found, ikeys = [own], [packed[key_width:]]
    for mine, theirs in blocks[1:]:
        *sums, ikey = other(turned, mine, theirs, lse, iturned, weight)
        found.append(sums)
        ikeys.append(ikey)
    sums = []
    for found_part, *_ in found:
        far = send(found_part.astype(BF16), 0, 2)
        summed = found_part + far.astype(F32)
        sums.append((summed, send(summed, 0, 1)))

    steps, grads = [], []
    for b in range(wide):
        grad_block = call(
            functools.partial(key_grad_kernel, b),
            (
                like((tokens, index_width), F32),
                like((tokens, iheads * tokens), BF16),
                like((tokens, tokens), F32),
            ),
            [vmem()] * 7,
            limit=8 << 20,
            flops=2 * tokens * tokens * iheads * index_width,
            moved=tokens * tokens * iheads * 6,
        )
        grad, coef, difference = grad_block(live, *sums[b], lse_row, found[b][1], weight, iquery)
        steps.append((coef, difference, found[b][1], ikeys[b]))
        if b:
            near = send(grad, 0, 1)
            grad = grad + near
        grads.append(grad.astype(BF16))

    far = send(grads[0], 0, 2)
    own_grad = grads[0].astype(F32) + far.astype(F32)
    shared = []
    for b in range(1, wide):
        shared.append(send(grads[b], b, 0, spread=True))
    own_grad = own_grad + send(own_grad, 0, 1)

    grad_query, grad_weight = call(
        functools.partial(query_grad_kernel, wide),
        (like((tokens, iheads * index_width), F32), like((iheads, tokens), F32)),
        [vmem()] * (4 * wide),
        limit=8 << 20,
        flops=2 * wide * tokens * tokens * iheads * index_width,
        moved=wide * tokens * tokens * iheads * 6,
    )(*(x for kind in zip(*steps) for x in kind))

    if wide == 1:
        return grad_query, grad_weight, own_grad
    shared = shared[0] if wide == 2 else sum(x.astype(F32) for x in shared)
    theirs = send(shared, 0, 1)
    return grad_query, grad_weight, own_grad + (shared.astype(F32) + theirs.astype(F32))


def solution(mesh):
    in_specs = (
        P(("seq", "wide"), "narrow"),
        P(("seq", "wide"), None),
        P("narrow", ("seq", "wide")),
        P(("seq", "wide"), "narrow"),
        P(("seq", "wide"), None),
        P("narrow", ("seq", "wide")),
        P(("seq", "wide")),
        P("seq"),
    )
    out_specs = (
        P(("seq", "wide"), "narrow"),
        P("narrow", ("seq", "wide")),
        P(("seq", "wide"), None),
    )
    return jax.shard_map(
        body,
        mesh=mesh,
        in_specs=in_specs,
        out_specs=out_specs,
        check_vma=False,
    )
```

```python
import functools
import math

import jax
import jax.numpy as jnp
from jax import lax
from jax.experimental import pallas as pl
from jax.experimental.pallas import tpu as pltpu
from jax.sharding import PartitionSpec as P


HEADS = 128
SPAN = 8
CHUNKS = 4
attn_scale = 192.0 ** (-0.5)
F32 = jnp.float32
BF16 = jnp.bfloat16


def vmem():
    return pl.BlockSpec(memory_space=pltpu.VMEM)


def call(kernel, out_shape, in_specs, scratch=(), limit=8 << 20, flops=0, moved=0):
    return pl.pallas_call(
        kernel,
        out_shape=out_shape,
        in_specs=in_specs,
        out_specs=jax.tree.map(lambda _: vmem(), out_shape),
        scratch_shapes=list(scratch),
        cost_estimate=pl.CostEstimate(flops=flops, bytes_accessed=moved, transcendentals=0),
        compiler_params=pltpu.CompilerParams(vmem_limit_bytes=limit),
    )


def side_by_side(refs):
    return jnp.concatenate([ref[...] for ref in refs], axis=1)


def index_sums(packed, iturned_ref, weight_ref, part_ref, active_ref):
    tokens, iheads = part_ref.shape[2], weight_ref.shape[0]
    index_width = iturned_ref.shape[0] // iheads
    index_scale = index_width ** (-0.5)
    score = 0.0
    for j in range(0, iheads, 2):
        rows = [iturned_ref.at[i * index_width : (i + 1) * index_width] for i in (j, j + 1)]
        logits = jnp.dot(
            packed[packed.shape[0] - tokens :], side_by_side(rows), preferred_element_type=F32
        )
        active = jnp.maximum(logits * index_scale, 0.0)
        active_ref[:, j * tokens : (j + 2) * tokens] = active
        for i in range(2):
            score = score + active[:, i * tokens : (i + 1) * tokens] * weight_ref[j + i : j + i + 1, :]
    part_ref[1] = score


def key_sides(packed, tokens):
    width = packed.shape[0] - tokens
    late = -width % 128
    if not late:
        return [jnp.transpose(packed[:width])] * 2
    fill = jnp.zeros((late, packed.shape[1]), BF16)
    orders = ((packed[:width], fill), (fill, packed[:width]))
    return [jnp.transpose(jnp.concatenate(parts, axis=0)) for parts in orders]


def pair_scores(turned, p, keys, side):
    pairs = [turned(p), turned(p + 1)]
    first = side * (pairs[0].shape[0] - keys.shape[1])
    rows = [pair.at[first : first + keys.shape[1]] for pair in pairs]
    return jnp.dot(keys, side_by_side(rows), preferred_element_type=F32)


def exp_sums(raw, p, side, lse_ref):
    tokens, total = lse_ref.shape[1], 0.0
    for i in range(2):
        h = 2 * (p + i) + side
        scores = raw[:, i * tokens : (i + 1) * tokens] * attn_scale
        total = total + jnp.exp(scores - lse_ref[h : h + 1, :])
    return total


def target_sums(turned, sides, lse_ref, part_ref):
    total = 0.0
    for p in range(0, lse_ref.shape[0] // 2, 2):
        for side, keys in enumerate(sides):
            total = total + exp_sums(pair_scores(turned, p, keys, side), p, side, lse_ref)
    part_ref[0] = total * (1.0 / HEADS)


def load_kernel(order_hbm, *refs):
    count = (len(refs) - 3) // 2
    sources, held = refs[:count], refs[count : 2 * count - 1]
    mine_ref, live_ref, order_ref, sems = refs[2 * count - 1 :]
    packed_ref = held[0]
    width = sources[0].shape[0]
    held = (packed_ref.at[:width], packed_ref.at[width:], *held[1:])
    moves = [
        pltpu.make_async_copy(src, dst, sems.at[i])
        for i, (src, dst) in enumerate(zip((order_hbm, *sources), (order_ref, *held)))
    ]
    for move in moves:
        move.start()
    for move in moves:
        move.wait()
    half = mine_ref.shape[0]
    core = lax.axis_index("narrow") % 2
    mine_ref[...] = packed_ref[pl.ds(pl.multiple_of(core * half, half), half)]

    place, blocks = lax.axis_index("wide"), live_ref.shape[0]
    for b in range(blocks):
        source = lax.rem(place - b + blocks, blocks)
        live = (order_ref[place] > order_ref[source]).astype(F32)
        live_ref[b] = jnp.full(live_ref.shape[1:], live, F32)


def own_kernel(
    query_hbm, packed_ref, iquery_ref, lse_ref, weight_ref,
    part_ref, active_ref, turned_ref, iturned_ref, query_ref, raw_ref, sems,
):
    pair_width = query_ref.shape[1] // lse_ref.shape[0] * 2
    tokens = part_ref.shape[2]
    step = query_ref.shape[1] // sems.shape[0]
    moves = []
    for i in range(sems.shape[0]):
        at = slice(i * step, (i + 1) * step)
        moves.append(pltpu.make_async_copy(query_hbm.at[:, at], query_ref.at[:, at], sems.at[i]))

    def turned(p):
        return turned_ref.at[p * pair_width : (p + 1) * pair_width]

    always = lax.axis_index("wide") >= 0
    moves[0].start()

    @pl.when(always)
    def _():
        index_width = iquery_ref.shape[1] // weight_ref.shape[0]
        for j in range(weight_ref.shape[0]):
            at = slice(j * index_width, (j + 1) * index_width)
            iturned_ref[at] = jnp.transpose(iquery_ref[:, at])

    for move in moves[1:2]:
        move.start()

    @pl.when(always)
    def _():
        index_sums(packed_ref, iturned_ref, weight_ref, part_ref, active_ref)

    for move in moves[2:]:
        move.start()

    @pl.when(always)
    def _():
        sides = key_sides(packed_ref, tokens)
        pairs = step // pair_width
        total = 0.0
        for i in range(len(moves) + 2):
            if i < len(moves):
                moves[i].wait()
                for p in range(i * pairs, (i + 1) * pairs):
                    at = slice(p * pair_width, (p + 1) * pair_width)
                    turned_ref[at] = jnp.transpose(query_ref[:, at])
            for lag in (1, 2):
                if not 0 <= i - lag < len(moves):
                    continue
                slot = (i - lag) % 2
                for k in range(pairs):
                    p, side = (i - lag) * pairs + k // 2 * 2, k % 2
                    if lag == 1:
                        raw_ref[slot, k] = pair_scores(turned, p, sides[side], side)
                    else:
                        total = total + exp_sums(raw_ref[slot, k], p, side, lse_ref)
        part_ref[0] = total * (1.0 / HEADS)


def other_kernel(
    turned_ref, mine_ref, theirs_ref, lse_ref, iturned_ref, weight_ref,
    part_ref, active_ref, ikey_ref, packed_ref,
):
    pair_width = turned_ref.shape[0] // lse_ref.shape[0] * 2
    half = mine_ref.shape[0]
    core = lax.axis_index("narrow") % 2
    packed_ref[pl.ds(pl.multiple_of(core * half, half), half)] = mine_ref[...]
    packed_ref[pl.ds(pl.multiple_of((1 - core) * half, half), half)] = theirs_ref[...]
    ikey_ref[...] = packed_ref[packed_ref.shape[0] - ikey_ref.shape[0] :]

    def turned(p):
        return turned_ref.at[p * pair_width : (p + 1) * pair_width]

    sides = key_sides(packed_ref, part_ref.shape[2])
    index_sums(packed_ref, iturned_ref, weight_ref, part_ref, active_ref)
    target_sums(turned, sides, lse_ref, part_ref)


def key_grad_kernel(
    step, live_ref, mine_ref, theirs_ref, lse_ref, active_ref, weight_ref, iquery_ref,
    grad_ref, coef_ref, diff_ref,
):
    keys, tokens = mine_ref.shape[1:]
    index_width = grad_ref.shape[1]
    iheads = weight_ref.shape[0]
    index_scale = index_width ** (-0.5)
    target = mine_ref[0] + theirs_ref[0]
    score = mine_ref[1] + theirs_ref[1]
    if step == 0:
        key_at = lax.broadcasted_iota(jnp.int32, (keys, tokens), 0)
        query_at = lax.broadcasted_iota(jnp.int32, (keys, tokens), 1)
        causal = query_at >= key_at
    else:
        causal = jnp.broadcast_to(live_ref[step], (keys, tokens)) > 0.0
    difference = jnp.where(causal, jnp.exp(score - lse_ref[...]) - target, 0.0)
    diff_ref[...] = difference
    total = jnp.zeros((keys, index_width), F32)
    span = math.gcd(iheads, SPAN)
    for first in range(0, iheads, span):
        for j in range(first, first + span):
            scaled = difference * (weight_ref[j : j + 1, :] * index_scale)
            coef = jnp.where(active_ref[:, j * tokens : (j + 1) * tokens] > 0.0, scaled, 0.0)
            coef_ref[:, j * tokens : (j + 1) * tokens] = coef.astype(BF16)
        rows = [
            iquery_ref[:, j * index_width : (j + 1) * index_width]
            for j in range(first, first + span)
        ]
        total = total + jnp.dot(
            coef_ref[:, first * tokens : (first + span) * tokens],
            jnp.concatenate(rows, axis=0),
            preferred_element_type=F32,
        )
    grad_ref[...] = total


def query_grad_kernel(blocks, *refs):
    coefs, diffs, actives, ikeys = (refs[i * blocks : (i + 1) * blocks] for i in range(4))
    grad_ref, weight_grad_ref = refs[4 * blocks :]
    tokens = diffs[0].shape[1]
    index_width = ikeys[0].shape[1]
    for j in range(weight_grad_ref.shape[0]):
        at = slice(j * tokens, (j + 1) * tokens)
        grad, weight_grad = 0.0, 0.0
        for coef, diff, active, ikey in zip(coefs, diffs, actives, ikeys):
            grad = grad + lax.dot_general(
                coef[:, at], ikey[...], (((0,), (0,)), ((), ())), preferred_element_type=F32
            )
            weight_grad = weight_grad + jnp.sum(diff[...] * active[:, at], axis=0, keepdims=True)
        grad_ref[:, j * index_width : (j + 1) * index_width] = grad
        weight_grad_ref[j : j + 1, :] = weight_grad


def body(
    attn_query, key_latent, lse_attn, index_query, index_key, index_weight, lse_index, block_order
):
    tokens, key_width = key_latent.shape
    index_width = index_key.shape[1]
    heads = attn_query.shape[1] // key_width
    iheads = index_query.shape[1] // index_width
    wide, narrow = lax.axis_size("wide"), lax.axis_size("narrow")
    ranks = range(wide * narrow)

    def send(block, step, flip, spread=False):
        route = []
        for r in ranks:
            turn = r % 2 * 2 if spread else flip
            route.append((r, (r // narrow - step) % wide * narrow + (r % narrow ^ turn)))
        return lax.ppermute(block, ("wide", "narrow"), route)

    like = jax.ShapeDtypeStruct
    hbm = pltpu.MemorySpace.HBM
    small = (
        jnp.transpose(key_latent),
        index_key,
        index_query,
        lse_attn,
        index_weight,
        lse_index[None, :],
    )
    half = (key_width + tokens) // 2
    packed, *small, mine, live = call(
        load_kernel,
        (like((key_width + tokens, tokens), BF16),)
        + tuple(like(a.shape, a.dtype) for a in small[2:])
        + (like((half, tokens), BF16), like((wide, 1, tokens), F32)),
        [pl.BlockSpec(memory_space=hbm)] * 7,
        [pltpu.SMEM(block_order.shape, jnp.int32), pltpu.SemaphoreType.DMA((7,))],
        limit=4 << 20,
    )(*(pltpu.with_memory_space_constraint(x, hbm) for x in (block_order, *small)))
    iquery, lse, weight, lse_row = small
    blocks = [None]
    for b in range(1, wide):
        first = send(mine, -b, 0)
        blocks.append((first, send(first, 0, 1)))

    part = like((2, tokens, tokens), F32)
    act = like((tokens, iheads * tokens), F32)
    work = dict(
        flops=2 * tokens * tokens * (heads * key_width + iheads * index_width),
        moved=attn_query.size * 2,
    )
    chunks = math.gcd(heads // 4, CHUNKS)
    *own, turned, iturned = call(
        own_kernel,
        (
            part,
            act,
            like((heads * key_width, tokens), BF16),
            like((iheads * index_width, tokens), BF16),
        ),
        [pl.BlockSpec(memory_space=hbm)] + [vmem()] * 4,
        [
            pltpu.VMEM(attn_query.shape, BF16),
            pltpu.VMEM((2, heads // 2 // chunks, tokens, 2 * tokens), F32),
            pltpu.SemaphoreType.DMA((chunks,)),
        ],
        limit=14 << 20,
        **work,
    )(pltpu.with_memory_space_constraint(attn_query, hbm), packed, iquery, lse, weight)
    other = call(
        other_kernel,
        (part, act, like(index_key.shape, BF16)),
        [vmem()] * 6,
        [pltpu.VMEM(packed.shape, BF16)],
        limit=10 << 20,
        **work,
    )
    found, ikeys = [own], [packed[key_width:]]
    for mine, theirs in blocks[1:]:
        *sums, ikey = other(turned, mine, theirs, lse, iturned, weight)
        found.append(sums)
        ikeys.append(ikey)
    sums = []
    for found_part, *_ in found:
        far = send(found_part.astype(BF16), 0, 2)
        summed = found_part + far.astype(F32)
        sums.append((summed, send(summed, 0, 1)))

    steps, grads = [], []
    for b in range(wide):
        grad_block = call(
            functools.partial(key_grad_kernel, b),
            (
                like((tokens, index_width), F32),
                like((tokens, iheads * tokens), BF16),
                like((tokens, tokens), F32),
            ),
            [vmem()] * 7,
            limit=8 << 20,
            flops=2 * tokens * tokens * iheads * index_width,
            moved=tokens * tokens * iheads * 6,
        )
        grad, coef, difference = grad_block(live, *sums[b], lse_row, found[b][1], weight, iquery)
        steps.append((coef, difference, found[b][1], ikeys[b]))
        if b:
            near = send(grad, 0, 1)
            grad = grad + near
        grads.append(grad.astype(BF16))

    far = send(grads[0], 0, 2)
    own_grad = grads[0].astype(F32) + far.astype(F32)
    shared = []
    for b in range(1, wide):
        shared.append(send(grads[b], b, 0, spread=True))
    own_grad = own_grad + send(own_grad, 0, 1)

    grad_query, grad_weight = call(
        functools.partial(query_grad_kernel, wide),
        (like((tokens, iheads * index_width), F32), like((iheads, tokens), F32)),
        [vmem()] * (4 * wide),
        limit=8 << 20,
        flops=2 * wide * tokens * tokens * iheads * index_width,
        moved=wide * tokens * tokens * iheads * 6,
    )(*(x for kind in zip(*steps) for x in kind))

    if wide == 1:
        return grad_query, grad_weight, own_grad
    shared = shared[0] if wide == 2 else sum(x.astype(F32) for x in shared)
    theirs = send(shared, 0, 1)
    return grad_query, grad_weight, own_grad + (shared.astype(F32) + theirs.astype(F32))


def solution(mesh):
    in_specs = (
        P(("seq", "wide"), "narrow"),
        P(("seq", "wide"), None),
        P("narrow", ("seq", "wide")),
        P(("seq", "wide"), "narrow"),
        P(("seq", "wide"), None),
        P("narrow", ("seq", "wide")),
        P(("seq", "wide")),
        P("seq"),
    )
    out_specs = (
        P(("seq", "wide"), "narrow"),
        P("narrow", ("seq", "wide")),
        P(("seq", "wide"), None),
    )
    return jax.shard_map(
        body,
        mesh=mesh,
        in_specs=in_specs,
        out_specs=out_specs,
        check_vma=False,
    )
```

```python
import functools
import math

import jax
import jax.numpy as jnp
from jax import lax
from jax.experimental import pallas as pl
from jax.experimental.pallas import tpu as pltpu
from jax.sharding import PartitionSpec as P


HEADS = 128
SPAN = 8
CHUNKS = 4
attn_scale = 192.0 ** (-0.5)
F32 = jnp.float32
BF16 = jnp.bfloat16


def vmem():
    return pl.BlockSpec(memory_space=pltpu.VMEM)


def call(kernel, out_shape, in_specs, scratch=(), limit=8 << 20, flops=0, moved=0):
    return pl.pallas_call(
        kernel,
        out_shape=out_shape,
        in_specs=in_specs,
        out_specs=jax.tree.map(lambda _: vmem(), out_shape),
        scratch_shapes=list(scratch),
        cost_estimate=pl.CostEstimate(flops=flops, bytes_accessed=moved, transcendentals=0),
        compiler_params=pltpu.CompilerParams(vmem_limit_bytes=limit),
    )


def side_by_side(refs):
    return jnp.concatenate([ref[...] for ref in refs], axis=1)


def index_sums(packed, iturned_ref, weight_ref, part_ref, active_ref):
    tokens, iheads = part_ref.shape[2], weight_ref.shape[0]
    index_width = iturned_ref.shape[0] // iheads
    index_scale = index_width ** (-0.5)
    score = 0.0
    for j in range(0, iheads, 2):
        rows = [iturned_ref.at[i * index_width : (i + 1) * index_width] for i in (j, j + 1)]
        logits = jnp.dot(
            packed[packed.shape[0] - tokens :], side_by_side(rows), preferred_element_type=F32
        )
        active = jnp.maximum(logits * index_scale, 0.0)
        active_ref[:, j * tokens : (j + 2) * tokens] = active
        for i in range(2):
            score = score + active[:, i * tokens : (i + 1) * tokens] * weight_ref[j + i : j + i + 1, :]
    part_ref[1] = score


def key_sides(packed, tokens):
    width = packed.shape[0] - tokens
    late = -width % 128
    if not late:
        return [jnp.transpose(packed[:width])] * 2
    fill = jnp.zeros((late, packed.shape[1]), BF16)
    orders = ((packed[:width], fill), (fill, packed[:width]))
    return [jnp.transpose(jnp.concatenate(parts, axis=0)) for parts in orders]


def pair_scores(turned, p, keys, side):
    pairs = [turned(p), turned(p + 1)]
    first = side * (pairs[0].shape[0] - keys.shape[1])
    rows = [pair.at[first : first + keys.shape[1]] for pair in pairs]
    return jnp.dot(keys, side_by_side(rows), preferred_element_type=F32)


def exp_sums(raw, p, side, lse_ref):
    tokens, total = lse_ref.shape[1], 0.0
    for i in range(2):
        h = 2 * (p + i) + side
        scores = raw[:, i * tokens : (i + 1) * tokens] * attn_scale
        total = total + jnp.exp(scores - lse_ref[h : h + 1, :])
    return total


def target_sums(turned, sides, lse_ref, part_ref):
    total = 0.0
    for p in range(0, lse_ref.shape[0] // 2, 2):
        for side, keys in enumerate(sides):
            total = total + exp_sums(pair_scores(turned, p, keys, side), p, side, lse_ref)
    part_ref[0] = total * (1.0 / HEADS)


def load_kernel(order_hbm, *refs):
    count = (len(refs) - 3) // 2
    sources, held = refs[:count], refs[count : 2 * count - 1]
    mine_ref, live_ref, order_ref, sems = refs[2 * count - 1 :]
    packed_ref = held[0]
    width = sources[0].shape[0]
    held = (packed_ref.at[:width], packed_ref.at[width:], *held[1:])
    moves = [
        pltpu.make_async_copy(src, dst, sems.at[i])
        for i, (src, dst) in enumerate(zip((order_hbm, *sources), (order_ref, *held)))
    ]
    for move in moves:
        move.start()
    for move in moves:
        move.wait()
    half = mine_ref.shape[0]
    core = lax.axis_index("narrow") % 2
    mine_ref[...] = packed_ref[pl.ds(pl.multiple_of(core * half, half), half)]

    place, blocks = lax.axis_index("wide"), live_ref.shape[0]
    for b in range(blocks):
        source = lax.rem(place - b + blocks, blocks)
        live = (order_ref[place] > order_ref[source]).astype(F32)
        live_ref[b] = jnp.full(live_ref.shape[1:], live, F32)


def own_kernel(
    query_hbm, packed_ref, iquery_ref, lse_ref, weight_ref,
    part_ref, active_ref, turned_ref, iturned_ref, query_ref, raw_ref, sems,
):
    pair_width = query_ref.shape[1] // lse_ref.shape[0] * 2
    tokens = part_ref.shape[2]
    step = query_ref.shape[1] // sems.shape[0]
    moves = []
    for i in range(sems.shape[0]):
        at = slice(i * step, (i + 1) * step)
        moves.append(pltpu.make_async_copy(query_hbm.at[:, at], query_ref.at[:, at], sems.at[i]))

    def turned(p):
        return turned_ref.at[p * pair_width : (p + 1) * pair_width]

    always = lax.axis_index("wide") >= 0
    moves[0].start()

    @pl.when(always)
    def _():
        index_width = iquery_ref.shape[1] // weight_ref.shape[0]
        for j in range(weight_ref.shape[0]):
            at = slice(j * index_width, (j + 1) * index_width)
            iturned_ref[at] = jnp.transpose(iquery_ref[:, at])

    for move in moves[1:2]:
        move.start()

    @pl.when(always)
    def _():
        index_sums(packed_ref, iturned_ref, weight_ref, part_ref, active_ref)

    for move in moves[2:]:
        move.start()

    @pl.when(always)
    def _():
        sides = key_sides(packed_ref, tokens)
        pairs = step // pair_width
        total = 0.0
        for i in range(len(moves) + 2):
            if i < len(moves):
                moves[i].wait()
                for p in range(i * pairs, (i + 1) * pairs):
                    at = slice(p * pair_width, (p + 1) * pair_width)
                    turned_ref[at] = jnp.transpose(query_ref[:, at])
            for lag in (1, 2):
                if not 0 <= i - lag < len(moves):
                    continue
                slot = (i - lag) % 2
                for k in range(pairs):
                    p, side = (i - lag) * pairs + k // 2 * 2, k % 2
                    if lag == 1:
                        raw_ref[slot, k] = pair_scores(turned, p, sides[side], side)
                    else:
                        total = total + exp_sums(raw_ref[slot, k], p, side, lse_ref)
        part_ref[0] = total * (1.0 / HEADS)


def other_kernel(
    turned_ref, mine_ref, theirs_ref, lse_ref, iturned_ref, weight_ref,
    part_ref, active_ref, ikey_ref, packed_ref,
):
    pair_width = turned_ref.shape[0] // lse_ref.shape[0] * 2
    half = mine_ref.shape[0]
    core = lax.axis_index("narrow") % 2
    packed_ref[pl.ds(pl.multiple_of(core * half, half), half)] = mine_ref[...]
    packed_ref[pl.ds(pl.multiple_of((1 - core) * half, half), half)] = theirs_ref[...]
    ikey_ref[...] = packed_ref[packed_ref.shape[0] - ikey_ref.shape[0] :]

    def turned(p):
        return turned_ref.at[p * pair_width : (p + 1) * pair_width]

    sides = key_sides(packed_ref, part_ref.shape[2])
    index_sums(packed_ref, iturned_ref, weight_ref, part_ref, active_ref)
    target_sums(turned, sides, lse_ref, part_ref)


def partner_kernel(
    ikey_ref, active_ref, iquery_ref, their_iquery_ref, actives_ref, iqueries_ref
):
    tokens, index_width = iquery_ref.shape[0], ikey_ref.shape[1]
    iheads = iquery_ref.shape[1] // index_width
    core = lax.axis_index("narrow") % 2
    iqueries_ref[core] = iquery_ref[...]
    iqueries_ref[1 - core] = their_iquery_ref[...]
    actives_ref[core] = active_ref[...]
    for j in range(0, iheads, 2):
        rows = [their_iquery_ref[:, i * index_width : (i + 1) * index_width] for i in (j, j + 1)]
        logits = lax.dot_general(
            ikey_ref[...],
            jnp.concatenate(rows, axis=0),
            (((1,), (1,)), ((), ())),
            preferred_element_type=F32,
        )
        actives_ref[1 - core, :, j * tokens : (j + 2) * tokens] = logits


def key_grad_kernel(
    step, live_ref, mine_ref, theirs_ref, lse_ref, weight_ref, actives_ref, iqueries_ref,
    grad_ref, coefs_ref, diff_ref,
):
    keys, tokens = diff_ref.shape
    index_width = grad_ref.shape[1]
    cores, iheads = coefs_ref.shape[0], coefs_ref.shape[2] // tokens
    index_scale = index_width ** (-0.5)
    target = mine_ref[:keys] + theirs_ref[:keys]
    score = mine_ref[keys : 2 * keys] + theirs_ref[keys : 2 * keys]
    weights = [weight_ref[...] * index_scale]
    if cores > 1:
        first_core = lax.axis_index("narrow") % 2 == 0
        weights.append(theirs_ref[2 * keys :] * index_scale)
        weights = [jnp.where(first_core, *w) for w in (weights, weights[::-1])]
    if step == 0:
        key_at = lax.broadcasted_iota(jnp.int32, (keys, tokens), 0)
        query_at = lax.broadcasted_iota(jnp.int32, (keys, tokens), 1)
        causal = query_at >= key_at
    else:
        causal = jnp.broadcast_to(live_ref[step], (keys, tokens)) > 0.0
    difference = jnp.where(causal, jnp.exp(score - lse_ref[...]) - target, 0.0)
    diff_ref[...] = difference
    total = jnp.zeros((keys, index_width), F32)
    span = math.gcd(iheads, SPAN)
    for c in range(cores):
        for first in range(0, iheads, span):
            for j in range(first, first + span):
                at = slice(j * tokens, (j + 1) * tokens)
                scaled = difference * weights[c][j : j + 1, :]
                coef = jnp.where(actives_ref[c, :, at] > 0.0, scaled, 0.0)
                coefs_ref[c, :, at] = coef.astype(BF16)
            rows = [
                iqueries_ref[c, :, j * index_width : (j + 1) * index_width]
                for j in range(first, first + span)
            ]
            total = total + jnp.dot(
                coefs_ref[c, :, first * tokens : (first + span) * tokens],
                jnp.concatenate(rows, axis=0),
                preferred_element_type=F32,
            )
    grad_ref[...] = total.astype(BF16)


def query_grad_kernel(blocks, *refs):
    coefs, diffs, actives, ikeys = (refs[i * blocks : (i + 1) * blocks] for i in range(4))
    grad_ref, weight_grad_ref = refs[4 * blocks :]
    tokens = diffs[0].shape[1]
    index_width = ikeys[0].shape[1]
    core = lax.axis_index("narrow") % 2
    for j in range(weight_grad_ref.shape[0]):
        at = slice(j * tokens, (j + 1) * tokens)
        grad, weight_grad = 0.0, 0.0
        for coef, diff, active, ikey in zip(coefs, diffs, actives, ikeys):
            grad = grad + lax.dot_general(
                coef[core if coef.shape[0] > 1 else 0, :, at], ikey[...], (((0,), (0,)), ((), ())), preferred_element_type=F32
            )
            weight_grad = weight_grad + jnp.sum(diff[...] * active[:, at], axis=0, keepdims=True)
        grad_ref[:, j * index_width : (j + 1) * index_width] = grad
        weight_grad_ref[j : j + 1, :] = weight_grad


def body(
    attn_query, key_latent, lse_attn, index_query, index_key, index_weight, lse_index, block_order
):
    tokens, key_width = key_latent.shape
    index_width = index_key.shape[1]
    heads = attn_query.shape[1] // key_width
    iheads = index_query.shape[1] // index_width
    wide, narrow = lax.axis_size("wide"), lax.axis_size("narrow")
    ranks = range(wide * narrow)

    def send(block, step, flip):
        route = [(r, (r // narrow - step) % wide * narrow + (r % narrow ^ flip)) for r in ranks]
        return lax.ppermute(block, ("wide", "narrow"), route)

    like = jax.ShapeDtypeStruct
    hbm = pltpu.MemorySpace.HBM
    small = (
        jnp.transpose(key_latent),
        index_key,
        index_query,
        lse_attn,
        index_weight,
        lse_index[None, :],
    )
    half = (key_width + tokens) // 2
    packed, *small, mine, live = call(
        load_kernel,
        (like((key_width + tokens, tokens), BF16),)
        + tuple(like(a.shape, a.dtype) for a in small[2:])
        + (like((half, tokens), BF16), like((wide, 1, tokens), F32)),
        [pl.BlockSpec(memory_space=hbm)] * 7,
        [pltpu.SMEM(block_order.shape, jnp.int32), pltpu.SemaphoreType.DMA((7,))],
        limit=4 << 20,
    )(*(pltpu.with_memory_space_constraint(x, hbm) for x in (block_order, *small)))
    iquery, lse, weight, lse_row = small
    their_iquery = send(index_query, 0, 1)
    blocks = [None]
    for b in range(1, wide):
        first = send(mine, -b, 0)
        blocks.append((first, send(first, 0, 1)))

    part = like((2, tokens, tokens), F32)
    act = like((tokens, iheads * tokens), F32)
    work = dict(
        flops=2 * tokens * tokens * (heads * key_width + iheads * index_width),
        moved=attn_query.size * 2,
    )
    chunks = math.gcd(heads // 4, CHUNKS)
    *own, turned, iturned = call(
        own_kernel,
        (
            part,
            act,
            like((heads * key_width, tokens), BF16),
            like((iheads * index_width, tokens), BF16),
        ),
        [pl.BlockSpec(memory_space=hbm)] + [vmem()] * 4,
        [
            pltpu.VMEM(attn_query.shape, BF16),
            pltpu.VMEM((2, heads // 2 // chunks, tokens, 2 * tokens), F32),
            pltpu.SemaphoreType.DMA((chunks,)),
        ],
        limit=14 << 20,
        **work,
    )(pltpu.with_memory_space_constraint(attn_query, hbm), packed, iquery, lse, weight)
    other = call(
        other_kernel,
        (part, act, like(index_key.shape, BF16)),
        [vmem()] * 6,
        [pltpu.VMEM(packed.shape, BF16)],
        limit=10 << 20,
        **work,
    )
    found, ikeys = [own], [packed[key_width:]]
    for mine, theirs in blocks[1:]:
        *sums, ikey = other(turned, mine, theirs, lse, iturned, weight)
        found.append(sums)
        ikeys.append(ikey)
    sums = []
    for b, (found_part, *_) in enumerate(found):
        far = send(found_part.astype(BF16), 0, 2)
        summed = jnp.reshape(found_part + far.astype(F32), (2 * tokens, tokens))
        if b:
            summed = jnp.concatenate([summed, weight], axis=0)
        sums.append((summed, send(summed, 0, 1)))

    steps, grads = [], []
    partner = call(
        partner_kernel,
        (
            like((2, tokens, iheads * tokens), F32),
            like((2, tokens, iheads * index_width), BF16),
        ),
        [vmem()] * 4,
        limit=8 << 20,
        flops=2 * tokens * tokens * iheads * index_width,
        moved=tokens * tokens * iheads * 12,
    )
    for b in range(wide):
        if b:
            both = partner(ikeys[b], found[b][1], iquery, their_iquery)
        else:
            both = (found[b][1][None], iquery[None])
        cores = both[0].shape[0]
        grad_block = call(
            functools.partial(key_grad_kernel, b),
            (
                like((tokens, index_width), BF16),
                like((cores, tokens, iheads * tokens), BF16),
                like((tokens, tokens), F32),
            ),
            [vmem()] * 7,
            limit=8 << 20,
            flops=2 * cores * tokens * tokens * iheads * index_width,
            moved=cores * tokens * tokens * iheads * 6,
        )
        grad, coef, difference = grad_block(live, *sums[b], lse_row, weight, *both)
        steps.append((coef, difference, found[b][1], ikeys[b]))
        grads.append(grad)

    far = send(grads[0], 0, 2)
    own_grad = grads[0].astype(F32) + far.astype(F32)
    others = 0.0
    for b in range(1, wide):
        cross = send(grads[b], b, 2)
        near = send(grads[b], b, 0)
        others = others + (near.astype(F32) + cross.astype(F32))
    own_grad = own_grad + send(own_grad, 0, 1)

    grad_query, grad_weight = call(
        functools.partial(query_grad_kernel, wide),
        (like((tokens, iheads * index_width), F32), like((iheads, tokens), F32)),
        [vmem()] * (4 * wide),
        limit=8 << 20,
        flops=2 * wide * tokens * tokens * iheads * index_width,
        moved=wide * tokens * tokens * iheads * 6,
    )(*(x for kind in zip(*steps) for x in kind))

    return grad_query, grad_weight, own_grad + others


def solution(mesh):
    in_specs = (
        P(("seq", "wide"), "narrow"),
        P(("seq", "wide"), None),
        P("narrow", ("seq", "wide")),
        P(("seq", "wide"), "narrow"),
        P(("seq", "wide"), None),
        P("narrow", ("seq", "wide")),
        P(("seq", "wide")),
        P("seq"),
    )
    out_specs = (
        P(("seq", "wide"), "narrow"),
        P("narrow", ("seq", "wide")),
        P(("seq", "wide"), None),
    )
    return jax.shard_map(
        body,
        mesh=mesh,
        in_specs=in_specs,
        out_specs=out_specs,
        check_vma=False,
    )
```

```python
import functools
import math

import jax
import jax.numpy as jnp
from jax import lax
from jax.experimental import pallas as pl
from jax.experimental.pallas import tpu as pltpu
from jax.sharding import PartitionSpec as P


HEADS = 128
SPAN = 8
CHUNKS = 4
attn_scale = 192.0 ** (-0.5)
F32 = jnp.float32
BF16 = jnp.bfloat16


def vmem():
    return pl.BlockSpec(memory_space=pltpu.VMEM)


def call(kernel, out_shape, in_specs, scratch=(), limit=8 << 20, flops=0, moved=0):
    return pl.pallas_call(
        kernel,
        out_shape=out_shape,
        in_specs=in_specs,
        out_specs=jax.tree.map(lambda _: vmem(), out_shape),
        scratch_shapes=list(scratch),
        cost_estimate=pl.CostEstimate(flops=flops, bytes_accessed=moved, transcendentals=0),
        compiler_params=pltpu.CompilerParams(vmem_limit_bytes=limit),
    )


def side_by_side(refs):
    return jnp.concatenate([ref[...] for ref in refs], axis=1)


def index_sums(packed, iturned_ref, weight_ref, part_ref, active_ref):
    tokens, iheads = part_ref.shape[2], weight_ref.shape[0]
    index_width = iturned_ref.shape[0] // iheads
    index_scale = index_width ** (-0.5)
    score = 0.0
    for j in range(0, iheads, 2):
        rows = [iturned_ref.at[i * index_width : (i + 1) * index_width] for i in (j, j + 1)]
        logits = jnp.dot(
            packed[packed.shape[0] - tokens :], side_by_side(rows), preferred_element_type=F32
        )
        active = jnp.maximum(logits * index_scale, 0.0)
        active_ref[:, j * tokens : (j + 2) * tokens] = active
        for i in range(2):
            score = score + active[:, i * tokens : (i + 1) * tokens] * weight_ref[j + i : j + i + 1, :]
    part_ref[1] = score


def key_sides(packed, tokens):
    width = packed.shape[0] - tokens
    late = -width % 128
    if not late:
        return [jnp.transpose(packed[:width])] * 2
    fill = jnp.zeros((late, packed.shape[1]), BF16)
    orders = ((packed[:width], fill), (fill, packed[:width]))
    return [jnp.transpose(jnp.concatenate(parts, axis=0)) for parts in orders]


def pair_scores(turned, p, keys, side):
    pairs = [turned(p), turned(p + 1)]
    first = side * (pairs[0].shape[0] - keys.shape[1])
    rows = [pair.at[first : first + keys.shape[1]] for pair in pairs]
    return jnp.dot(keys, side_by_side(rows), preferred_element_type=F32)


def exp_sums(raw, p, side, lse_ref):
    tokens, total = lse_ref.shape[1], 0.0
    for i in range(2):
        h = 2 * (p + i) + side
        scores = raw[:, i * tokens : (i + 1) * tokens] * attn_scale
        total = total + jnp.exp(scores - lse_ref[h : h + 1, :])
    return total


def target_sums(turned, sides, lse_ref, part_ref):
    total = 0.0
    for p in range(0, lse_ref.shape[0] // 2, 2):
        for side, keys in enumerate(sides):
            total = total + exp_sums(pair_scores(turned, p, keys, side), p, side, lse_ref)
    part_ref[0] = total * (1.0 / HEADS)


def load_kernel(order_hbm, *refs):
    count = (len(refs) - 3) // 2
    sources, held = refs[:count], refs[count : 2 * count - 1]
    mine_ref, live_ref, order_ref, sems = refs[2 * count - 1 :]
    packed_ref = held[0]
    width = sources[0].shape[0]
    held = (packed_ref.at[:width], packed_ref.at[width:], *held[1:])
    moves = [
        pltpu.make_async_copy(src, dst, sems.at[i])
        for i, (src, dst) in enumerate(zip((order_hbm, *sources), (order_ref, *held)))
    ]
    for move in moves:
        move.start()
    for move in moves:
        move.wait()
    half = mine_ref.shape[0]
    core = lax.axis_index("narrow") % 2
    mine_ref[...] = packed_ref[pl.ds(pl.multiple_of(core * half, half), half)]

    place, blocks = lax.axis_index("wide"), live_ref.shape[0]
    for b in range(blocks):
        source = lax.rem(place - b + blocks, blocks)
        live = (order_ref[place] > order_ref[source]).astype(F32)
        live_ref[b] = jnp.full(live_ref.shape[1:], live, F32)


def own_kernel(
    query_hbm, packed_ref, iquery_ref, lse_ref, weight_ref,
    part_ref, active_ref, turned_ref, iturned_ref, query_ref, raw_ref, sems,
):
    pair_width = query_ref.shape[1] // lse_ref.shape[0] * 2
    tokens = part_ref.shape[2]
    step = query_ref.shape[1] // sems.shape[0]
    moves = []
    for i in range(sems.shape[0]):
        at = slice(i * step, (i + 1) * step)
        moves.append(pltpu.make_async_copy(query_hbm.at[:, at], query_ref.at[:, at], sems.at[i]))

    def turned(p):
        return turned_ref.at[p * pair_width : (p + 1) * pair_width]

    always = lax.axis_index("wide") >= 0
    moves[0].start()

    @pl.when(always)
    def _():
        index_width = iquery_ref.shape[1] // weight_ref.shape[0]
        for j in range(weight_ref.shape[0]):
            at = slice(j * index_width, (j + 1) * index_width)
            iturned_ref[at] = jnp.transpose(iquery_ref[:, at])

    for move in moves[1:2]:
        move.start()

    @pl.when(always)
    def _():
        index_sums(packed_ref, iturned_ref, weight_ref, part_ref, active_ref)

    for move in moves[2:]:
        move.start()

    @pl.when(always)
    def _():
        sides = key_sides(packed_ref, tokens)
        pairs = step // pair_width
        total = 0.0
        for i in range(len(moves) + 2):
            if i < len(moves):
                moves[i].wait()
                for p in range(i * pairs, (i + 1) * pairs):
                    at = slice(p * pair_width, (p + 1) * pair_width)
                    turned_ref[at] = jnp.transpose(query_ref[:, at])
            for lag in (1, 2):
                if not 0 <= i - lag < len(moves):
                    continue
                slot = (i - lag) % 2
                for k in range(pairs):
                    p, side = (i - lag) * pairs + k // 2 * 2, k % 2
                    if lag == 1:
                        raw_ref[slot, k] = pair_scores(turned, p, sides[side], side)
                    else:
                        total = total + exp_sums(raw_ref[slot, k], p, side, lse_ref)
        part_ref[0] = total * (1.0 / HEADS)


def other_kernel(
    turned_ref, mine_ref, theirs_ref, lse_ref, iturned_ref, weight_ref,
    part_ref, active_ref, ikey_ref, packed_ref,
):
    pair_width = turned_ref.shape[0] // lse_ref.shape[0] * 2
    half = mine_ref.shape[0]
    core = lax.axis_index("narrow") % 2
    packed_ref[pl.ds(pl.multiple_of(core * half, half), half)] = mine_ref[...]
    packed_ref[pl.ds(pl.multiple_of((1 - core) * half, half), half)] = theirs_ref[...]
    ikey_ref[...] = packed_ref[packed_ref.shape[0] - ikey_ref.shape[0] :]

    def turned(p):
        return turned_ref.at[p * pair_width : (p + 1) * pair_width]

    sides = key_sides(packed_ref, part_ref.shape[2])
    index_sums(packed_ref, iturned_ref, weight_ref, part_ref, active_ref)
    target_sums(turned, sides, lse_ref, part_ref)


def partner_kernel(
    ikey_ref, active_ref, iquery_ref, their_iquery_ref, actives_ref, iqueries_ref
):
    tokens, index_width = iquery_ref.shape[0], ikey_ref.shape[1]
    iheads = iquery_ref.shape[1] // index_width
    core = lax.axis_index("narrow") % 2
    iqueries_ref[core] = iquery_ref[...]
    iqueries_ref[1 - core] = their_iquery_ref[...]
    actives_ref[core] = active_ref[...]
    for j in range(0, iheads, 2):
        rows = [their_iquery_ref[:, i * index_width : (i + 1) * index_width] for i in (j, j + 1)]
        logits = lax.dot_general(
            ikey_ref[...],
            jnp.concatenate(rows, axis=0),
            (((1,), (1,)), ((), ())),
            preferred_element_type=F32,
        )
        actives_ref[1 - core, :, j * tokens : (j + 2) * tokens] = logits


def key_grad_kernel(
    step, live_ref, mine_ref, theirs_ref, lse_ref, weight_ref, actives_ref, iqueries_ref,
    grad_ref, coefs_ref, diff_ref,
):
    keys, tokens = diff_ref.shape
    index_width = grad_ref.shape[1]
    cores, iheads = coefs_ref.shape[0], coefs_ref.shape[2] // tokens
    index_scale = index_width ** (-0.5)
    target = mine_ref[:keys] + theirs_ref[:keys]
    score = mine_ref[keys : 2 * keys] + theirs_ref[keys : 2 * keys]
    weights = [weight_ref[...] * index_scale]
    if cores > 1:
        first_core = lax.axis_index("narrow") % 2 == 0
        weights.append(theirs_ref[2 * keys :] * index_scale)
        weights = [jnp.where(first_core, *w) for w in (weights, weights[::-1])]
    if step == 0:
        key_at = lax.broadcasted_iota(jnp.int32, (keys, tokens), 0)
        query_at = lax.broadcasted_iota(jnp.int32, (keys, tokens), 1)
        causal = query_at >= key_at
    else:
        causal = jnp.broadcast_to(live_ref[step], (keys, tokens)) > 0.0
    difference = jnp.where(causal, jnp.exp(score - lse_ref[...]) - target, 0.0)
    diff_ref[...] = difference
    total = jnp.zeros((keys, index_width), F32)
    span = math.gcd(iheads, SPAN)
    for c in range(cores):
        for first in range(0, iheads, span):
            for j in range(first, first + span):
                at = slice(j * tokens, (j + 1) * tokens)
                scaled = difference * weights[c][j : j + 1, :]
                coef = jnp.where(actives_ref[c, :, at] > 0.0, scaled, 0.0)
                coefs_ref[c, :, at] = coef.astype(BF16)
            rows = [
                iqueries_ref[c, :, j * index_width : (j + 1) * index_width]
                for j in range(first, first + span)
            ]
            total = total + jnp.dot(
                coefs_ref[c, :, first * tokens : (first + span) * tokens],
                jnp.concatenate(rows, axis=0),
                preferred_element_type=F32,
            )
    grad_ref[...] = total.astype(BF16)


def split(part):
    high = lax.reduce_precision(part[1], 8, 7)
    return jnp.stack([part[0], high, part[1] - high]).astype(BF16)


def received(pieces):
    pieces = pieces.astype(F32)
    return jnp.stack([pieces[0], pieces[1] + pieces[2]])


def query_grad_kernel(blocks, *refs):
    coefs, diffs, actives, ikeys = (refs[i * blocks : (i + 1) * blocks] for i in range(4))
    grad_ref, weight_grad_ref = refs[4 * blocks :]
    tokens = diffs[0].shape[1]
    index_width = ikeys[0].shape[1]
    core = lax.axis_index("narrow") % 2
    for j in range(weight_grad_ref.shape[0]):
        at = slice(j * tokens, (j + 1) * tokens)
        grad, weight_grad = 0.0, 0.0
        for coef, diff, active, ikey in zip(coefs, diffs, actives, ikeys):
            grad = grad + lax.dot_general(
                coef[core if coef.shape[0] > 1 else 0, :, at], ikey[...], (((0,), (0,)), ((), ())), preferred_element_type=F32
            )
            weight_grad = weight_grad + jnp.sum(diff[...] * active[:, at], axis=0, keepdims=True)
        grad_ref[:, j * index_width : (j + 1) * index_width] = grad
        weight_grad_ref[j : j + 1, :] = weight_grad


def body(
    attn_query, key_latent, lse_attn, index_query, index_key, index_weight, lse_index, block_order
):
    tokens, key_width = key_latent.shape
    index_width = index_key.shape[1]
    heads = attn_query.shape[1] // key_width
    iheads = index_query.shape[1] // index_width
    wide, narrow = lax.axis_size("wide"), lax.axis_size("narrow")
    ranks = range(wide * narrow)

    def send(block, step, flip):
        route = [(r, (r // narrow - step) % wide * narrow + (r % narrow ^ flip)) for r in ranks]
        return lax.ppermute(block, ("wide", "narrow"), route)

    like = jax.ShapeDtypeStruct
    hbm = pltpu.MemorySpace.HBM
    small = (
        jnp.transpose(key_latent),
        index_key,
        index_query,
        lse_attn,
        index_weight,
        lse_index[None, :],
    )
    half = (key_width + tokens) // 2
    packed, *small, mine, live = call(
        load_kernel,
        (like((key_width + tokens, tokens), BF16),)
        + tuple(like(a.shape, a.dtype) for a in small[2:])
        + (like((half, tokens), BF16), like((wide, 1, tokens), F32)),
        [pl.BlockSpec(memory_space=hbm)] * 7,
        [pltpu.SMEM(block_order.shape, jnp.int32), pltpu.SemaphoreType.DMA((7,))],
        limit=4 << 20,
    )(*(pltpu.with_memory_space_constraint(x, hbm) for x in (block_order, *small)))
    iquery, lse, weight, lse_row = small
    their_iquery = send(index_query, 0, 1)
    blocks = [None]
    for b in range(1, wide):
        first = send(mine, -b, 0)
        blocks.append((first, send(first, 0, 1)))

    part = like((2, tokens, tokens), F32)
    act = like((tokens, iheads * tokens), F32)
    work = dict(
        flops=2 * tokens * tokens * (heads * key_width + iheads * index_width),
        moved=attn_query.size * 2,
    )
    chunks = math.gcd(heads // 4, CHUNKS)
    *own, turned, iturned = call(
        own_kernel,
        (
            part,
            act,
            like((heads * key_width, tokens), BF16),
            like((iheads * index_width, tokens), BF16),
        ),
        [pl.BlockSpec(memory_space=hbm)] + [vmem()] * 4,
        [
            pltpu.VMEM(attn_query.shape, BF16),
            pltpu.VMEM((2, heads // 2 // chunks, tokens, 2 * tokens), F32),
            pltpu.SemaphoreType.DMA((chunks,)),
        ],
        limit=14 << 20,
        **work,
    )(pltpu.with_memory_space_constraint(attn_query, hbm), packed, iquery, lse, weight)
    other = call(
        other_kernel,
        (part, act, like(index_key.shape, BF16)),
        [vmem()] * 6,
        [pltpu.VMEM(packed.shape, BF16)],
        limit=10 << 20,
        **work,
    )
    found, ikeys = [own], [packed[key_width:]]
    for mine, theirs in blocks[1:]:
        *sums, ikey = other(turned, mine, theirs, lse, iturned, weight)
        found.append(sums)
        ikeys.append(ikey)
    sums = []
    for b, (found_part, *_) in enumerate(found):
        far = received(send(split(found_part), 0, 2))
        summed = jnp.reshape(found_part + far, (2 * tokens, tokens))
        if b:
            summed = jnp.concatenate([summed, weight], axis=0)
        sums.append((summed, send(summed, 0, 1)))

    steps, grads = [], []
    partner = call(
        partner_kernel,
        (
            like((2, tokens, iheads * tokens), F32),
            like((2, tokens, iheads * index_width), BF16),
        ),
        [vmem()] * 4,
        limit=8 << 20,
        flops=2 * tokens * tokens * iheads * index_width,
        moved=tokens * tokens * iheads * 12,
    )
    for b in range(wide):
        if b:
            both = partner(ikeys[b], found[b][1], iquery, their_iquery)
        else:
            both = (found[b][1][None], iquery[None])
        cores = both[0].shape[0]
        grad_block = call(
            functools.partial(key_grad_kernel, b),
            (
                like((tokens, index_width), BF16),
                like((cores, tokens, iheads * tokens), BF16),
                like((tokens, tokens), F32),
            ),
            [vmem()] * 7,
            limit=8 << 20,
            flops=2 * cores * tokens * tokens * iheads * index_width,
            moved=cores * tokens * tokens * iheads * 6,
        )
        grad, coef, difference = grad_block(live, *sums[b], lse_row, weight, *both)
        steps.append((coef, difference, found[b][1], ikeys[b]))
        grads.append(grad)

    far = send(grads[0], 0, 2)
    own_grad = grads[0].astype(F32) + far.astype(F32)
    others = 0.0
    for b in range(1, wide):
        cross = send(grads[b], b, 2)
        near = send(grads[b], b, 0)
        others = others + (near.astype(F32) + cross.astype(F32))
    own_grad = own_grad + send(own_grad, 0, 1)

    grad_query, grad_weight = call(
        functools.partial(query_grad_kernel, wide),
        (like((tokens, iheads * index_width), F32), like((iheads, tokens), F32)),
        [vmem()] * (4 * wide),
        limit=8 << 20,
        flops=2 * wide * tokens * tokens * iheads * index_width,
        moved=wide * tokens * tokens * iheads * 6,
    )(*(x for kind in zip(*steps) for x in kind))

    return grad_query, grad_weight, own_grad + others


def solution(mesh):
    in_specs = (
        P(("seq", "wide"), "narrow"),
        P(("seq", "wide"), None),
        P("narrow", ("seq", "wide")),
        P(("seq", "wide"), "narrow"),
        P(("seq", "wide"), None),
        P("narrow", ("seq", "wide")),
        P(("seq", "wide")),
        P("seq"),
    )
    out_specs = (
        P(("seq", "wide"), "narrow"),
        P("narrow", ("seq", "wide")),
        P(("seq", "wide"), None),
    )
    return jax.shard_map(
        body,
        mesh=mesh,
        in_specs=in_specs,
        out_specs=out_specs,
        check_vma=False,
    )
```

```python
import functools
import math

import jax
import jax.numpy as jnp
from jax import lax
from jax.experimental import pallas as pl
from jax.experimental.pallas import tpu as pltpu
from jax.sharding import PartitionSpec as P


HEADS = 128
SPAN = 8
CHUNKS = 4
attn_scale = 192.0 ** (-0.5)
F32 = jnp.float32
BF16 = jnp.bfloat16


def vmem():
    return pl.BlockSpec(memory_space=pltpu.VMEM)


def call(kernel, out_shape, in_specs, scratch=(), limit=8 << 20, flops=0, moved=0):
    return pl.pallas_call(
        kernel,
        out_shape=out_shape,
        in_specs=in_specs,
        out_specs=jax.tree.map(lambda _: vmem(), out_shape),
        scratch_shapes=list(scratch),
        cost_estimate=pl.CostEstimate(flops=flops, bytes_accessed=moved, transcendentals=0),
        compiler_params=pltpu.CompilerParams(vmem_limit_bytes=limit),
    )


def side_by_side(refs):
    return jnp.concatenate([ref[...] for ref in refs], axis=1)


def index_sums(packed, iturned_ref, weight_ref, part_ref, active_ref):
    tokens, iheads = part_ref.shape[2], weight_ref.shape[0]
    index_width = iturned_ref.shape[0] // iheads
    index_scale = index_width ** (-0.5)
    score = 0.0
    for j in range(0, iheads, 2):
        rows = [iturned_ref.at[i * index_width : (i + 1) * index_width] for i in (j, j + 1)]
        logits = jnp.dot(
            packed[packed.shape[0] - tokens :], side_by_side(rows), preferred_element_type=F32
        )
        active = jnp.maximum(logits * index_scale, 0.0)
        active_ref[:, j * tokens : (j + 2) * tokens] = active
        for i in range(2):
            score = score + active[:, i * tokens : (i + 1) * tokens] * weight_ref[j + i : j + i + 1, :]
    part_ref[1] = score


def key_sides(packed, tokens):
    width = packed.shape[0] - tokens
    late = -width % 128
    if not late:
        return [jnp.transpose(packed[:width])] * 2
    fill = jnp.zeros((late, packed.shape[1]), BF16)
    orders = ((packed[:width], fill), (fill, packed[:width]))
    return [jnp.transpose(jnp.concatenate(parts, axis=0)) for parts in orders]


def pair_scores(turned, p, keys, side):
    pairs = [turned(p), turned(p + 1)]
    first = side * (pairs[0].shape[0] - keys.shape[1])
    rows = [pair.at[first : first + keys.shape[1]] for pair in pairs]
    return jnp.dot(keys, side_by_side(rows), preferred_element_type=F32)


def exp_sums(raw, p, side, lse_ref):
    tokens, total = lse_ref.shape[1], 0.0
    for i in range(2):
        h = 2 * (p + i) + side
        scores = raw[:, i * tokens : (i + 1) * tokens] * attn_scale
        total = total + jnp.exp(scores - lse_ref[h : h + 1, :])
    return total


def target_sums(turned, sides, lse_ref, part_ref):
    total = 0.0
    for p in range(0, lse_ref.shape[0] // 2, 2):
        for side, keys in enumerate(sides):
            total = total + exp_sums(pair_scores(turned, p, keys, side), p, side, lse_ref)
    part_ref[0] = total * (1.0 / HEADS)


def load_kernel(order_hbm, *refs):
    count = (len(refs) - 3) // 2
    sources, held = refs[:count], refs[count : 2 * count - 1]
    mine_ref, live_ref, order_ref, sems = refs[2 * count - 1 :]
    packed_ref = held[0]
    width = sources[0].shape[0]
    held = (packed_ref.at[:width], packed_ref.at[width:], *held[1:])
    moves = [
        pltpu.make_async_copy(src, dst, sems.at[i])
        for i, (src, dst) in enumerate(zip((order_hbm, *sources), (order_ref, *held)))
    ]
    for move in moves:
        move.start()
    for move in moves:
        move.wait()
    half = mine_ref.shape[0]
    core = lax.axis_index("narrow") % 2
    mine_ref[...] = packed_ref[pl.ds(pl.multiple_of(core * half, half), half)]

    place, blocks = lax.axis_index("wide"), live_ref.shape[0]
    for b in range(blocks):
        source = lax.rem(place - b + blocks, blocks)
        live = (order_ref[place] > order_ref[source]).astype(F32)
        live_ref[b] = jnp.full(live_ref.shape[1:], live, F32)


def own_kernel(
    query_hbm, packed_ref, iquery_ref, lse_ref, weight_ref,
    part_ref, active_ref, turned_ref, iturned_ref, query_ref, raw_ref, sems,
):
    pair_width = query_ref.shape[1] // lse_ref.shape[0] * 2
    tokens = part_ref.shape[2]
    step = query_ref.shape[1] // sems.shape[0]
    moves = []
    for i in range(sems.shape[0]):
        at = slice(i * step, (i + 1) * step)
        moves.append(pltpu.make_async_copy(query_hbm.at[:, at], query_ref.at[:, at], sems.at[i]))

    def turned(p):
        return turned_ref.at[p * pair_width : (p + 1) * pair_width]

    always = lax.axis_index("wide") >= 0
    moves[0].start()

    @pl.when(always)
    def _():
        index_width = iquery_ref.shape[1] // weight_ref.shape[0]
        for j in range(weight_ref.shape[0]):
            at = slice(j * index_width, (j + 1) * index_width)
            iturned_ref[at] = jnp.transpose(iquery_ref[:, at])

    for move in moves[1:2]:
        move.start()

    @pl.when(always)
    def _():
        index_sums(packed_ref, iturned_ref, weight_ref, part_ref, active_ref)

    for move in moves[2:]:
        move.start()

    @pl.when(always)
    def _():
        sides = key_sides(packed_ref, tokens)
        pairs = step // pair_width
        total = 0.0
        for i in range(len(moves) + 2):
            if i < len(moves):
                moves[i].wait()
                for p in range(i * pairs, (i + 1) * pairs):
                    at = slice(p * pair_width, (p + 1) * pair_width)
                    turned_ref[at] = jnp.transpose(query_ref[:, at])
            for lag in (1, 2):
                if not 0 <= i - lag < len(moves):
                    continue
                slot = (i - lag) % 2
                for k in range(pairs):
                    p, side = (i - lag) * pairs + k // 2 * 2, k % 2
                    if lag == 1:
                        raw_ref[slot, k] = pair_scores(turned, p, sides[side], side)
                    else:
                        total = total + exp_sums(raw_ref[slot, k], p, side, lse_ref)
        part_ref[0] = total * (1.0 / HEADS)


def other_kernel(
    turned_ref, mine_ref, theirs_ref, lse_ref, iturned_ref, weight_ref,
    part_ref, active_ref, ikey_ref, packed_ref,
):
    pair_width = turned_ref.shape[0] // lse_ref.shape[0] * 2
    half = mine_ref.shape[0]
    core = lax.axis_index("narrow") % 2
    packed_ref[pl.ds(pl.multiple_of(core * half, half), half)] = mine_ref[...]
    packed_ref[pl.ds(pl.multiple_of((1 - core) * half, half), half)] = theirs_ref[...]
    ikey_ref[...] = packed_ref[packed_ref.shape[0] - ikey_ref.shape[0] :]

    def turned(p):
        return turned_ref.at[p * pair_width : (p + 1) * pair_width]

    sides = key_sides(packed_ref, part_ref.shape[2])
    index_sums(packed_ref, iturned_ref, weight_ref, part_ref, active_ref)
    target_sums(turned, sides, lse_ref, part_ref)


def partner_kernel(
    ikey_ref, active_ref, iquery_ref, their_iquery_ref, actives_ref, iqueries_ref
):
    tokens, index_width = iquery_ref.shape[0], ikey_ref.shape[1]
    iheads = iquery_ref.shape[1] // index_width
    core = lax.axis_index("narrow") % 2
    iqueries_ref[core] = iquery_ref[...]
    iqueries_ref[1 - core] = their_iquery_ref[...]
    actives_ref[core] = active_ref[...]
    for j in range(0, iheads, 2):
        rows = [their_iquery_ref[:, i * index_width : (i + 1) * index_width] for i in (j, j + 1)]
        logits = lax.dot_general(
            ikey_ref[...],
            jnp.concatenate(rows, axis=0),
            (((1,), (1,)), ((), ())),
            preferred_element_type=F32,
        )
        actives_ref[1 - core, :, j * tokens : (j + 2) * tokens] = logits


def key_grad_kernel(
    step, live_ref, mine_ref, theirs_ref, lse_ref, weight_ref, actives_ref, iqueries_ref,
    grad_ref, coefs_ref, diff_ref,
):
    keys, tokens = diff_ref.shape
    index_width = grad_ref.shape[1]
    cores, iheads = coefs_ref.shape[0], coefs_ref.shape[2] // tokens
    index_scale = index_width ** (-0.5)
    target = mine_ref[:keys] + theirs_ref[:keys]
    score = mine_ref[keys : 2 * keys] + theirs_ref[keys : 2 * keys]
    weights = [weight_ref[...] * index_scale]
    if cores > 1:
        first_core = lax.axis_index("narrow") % 2 == 0
        weights.append(theirs_ref[2 * keys :] * index_scale)
        weights = [jnp.where(first_core, *w) for w in (weights, weights[::-1])]
    if step == 0:
        key_at = lax.broadcasted_iota(jnp.int32, (keys, tokens), 0)
        query_at = lax.broadcasted_iota(jnp.int32, (keys, tokens), 1)
        causal = query_at >= key_at
    else:
        causal = jnp.broadcast_to(live_ref[step], (keys, tokens)) > 0.0
    difference = jnp.where(causal, jnp.exp(score - lse_ref[...]) - target, 0.0)
    diff_ref[...] = difference
    total = jnp.zeros((keys, index_width), F32)
    span = math.gcd(iheads, SPAN)
    for c in range(cores):
        for first in range(0, iheads, span):
            for j in range(first, first + span):
                at = slice(j * tokens, (j + 1) * tokens)
                scaled = difference * weights[c][j : j + 1, :]
                coef = jnp.where(actives_ref[c, :, at] > 0.0, scaled, 0.0)
                coefs_ref[c, :, at] = coef.astype(BF16)
            rows = [
                iqueries_ref[c, :, j * index_width : (j + 1) * index_width]
                for j in range(first, first + span)
            ]
            total = total + jnp.dot(
                coefs_ref[c, :, first * tokens : (first + span) * tokens],
                jnp.concatenate(rows, axis=0),
                preferred_element_type=F32,
            )
    grad_ref[...] = total.astype(BF16)


def split(part):
    high = lax.reduce_precision(part[1], 8, 7)
    return jnp.stack([part[0], high, part[1] - high]).astype(BF16)


def query_grad_kernel(blocks, *refs):
    coefs, diffs, actives, ikeys = (refs[i * blocks : (i + 1) * blocks] for i in range(4))
    grad_ref, weight_grad_ref = refs[4 * blocks :]
    tokens = diffs[0].shape[1]
    index_width = ikeys[0].shape[1]
    core = lax.axis_index("narrow") % 2
    for j in range(weight_grad_ref.shape[0]):
        at = slice(j * tokens, (j + 1) * tokens)
        grad, weight_grad = 0.0, 0.0
        for coef, diff, active, ikey in zip(coefs, diffs, actives, ikeys):
            grad = grad + lax.dot_general(
                coef[core if coef.shape[0] > 1 else 0, :, at], ikey[...], (((0,), (0,)), ((), ())), preferred_element_type=F32
            )
            weight_grad = weight_grad + jnp.sum(diff[...] * active[:, at], axis=0, keepdims=True)
        grad_ref[:, j * index_width : (j + 1) * index_width] = grad
        weight_grad_ref[j : j + 1, :] = weight_grad


def body(
    attn_query, key_latent, lse_attn, index_query, index_key, index_weight, lse_index, block_order
):
    tokens, key_width = key_latent.shape
    index_width = index_key.shape[1]
    heads = attn_query.shape[1] // key_width
    iheads = index_query.shape[1] // index_width
    wide, narrow = lax.axis_size("wide"), lax.axis_size("narrow")
    ranks = range(wide * narrow)

    def send(block, step, flip):
        route = [(r, (r // narrow - step) % wide * narrow + (r % narrow ^ flip)) for r in ranks]
        return lax.ppermute(block, ("wide", "narrow"), route)

    like = jax.ShapeDtypeStruct
    hbm = pltpu.MemorySpace.HBM
    small = (
        jnp.transpose(key_latent),
        index_key,
        index_query,
        lse_attn,
        index_weight,
        lse_index[None, :],
    )
    half = (key_width + tokens) // 2
    packed, *small, mine, live = call(
        load_kernel,
        (like((key_width + tokens, tokens), BF16),)
        + tuple(like(a.shape, a.dtype) for a in small[2:])
        + (like((half, tokens), BF16), like((wide, 1, tokens), F32)),
        [pl.BlockSpec(memory_space=hbm)] * 7,
        [pltpu.SMEM(block_order.shape, jnp.int32), pltpu.SemaphoreType.DMA((7,))],
        limit=4 << 20,
    )(*(pltpu.with_memory_space_constraint(x, hbm) for x in (block_order, *small)))
    iquery, lse, weight, lse_row = small
    their_iquery = send(index_query, 0, 1)
    blocks = [None]
    for b in range(1, wide):
        first = send(mine, -b, 0)
        blocks.append((first, send(first, 0, 1)))

    part = like((2, tokens, tokens), F32)
    act = like((tokens, iheads * tokens), F32)
    work = dict(
        flops=2 * tokens * tokens * (heads * key_width + iheads * index_width),
        moved=attn_query.size * 2,
    )
    chunks = math.gcd(heads // 4, CHUNKS)
    *own, turned, iturned = call(
        own_kernel,
        (
            part,
            act,
            like((heads * key_width, tokens), BF16),
            like((iheads * index_width, tokens), BF16),
        ),
        [pl.BlockSpec(memory_space=hbm)] + [vmem()] * 4,
        [
            pltpu.VMEM(attn_query.shape, BF16),
            pltpu.VMEM((2, heads // 2 // chunks, tokens, 2 * tokens), F32),
            pltpu.SemaphoreType.DMA((chunks,)),
        ],
        limit=14 << 20,
        **work,
    )(pltpu.with_memory_space_constraint(attn_query, hbm), packed, iquery, lse, weight)
    other = call(
        other_kernel,
        (part, act, like(index_key.shape, BF16)),
        [vmem()] * 6,
        [pltpu.VMEM(packed.shape, BF16)],
        limit=10 << 20,
        **work,
    )
    found, ikeys = [own], [packed[key_width:]]
    for mine, theirs in blocks[1:]:
        *sums, ikey = other(turned, mine, theirs, lse, iturned, weight)
        found.append(sums)
        ikeys.append(ikey)
    sums = []
    for b, (found_part, *_) in enumerate(found):
        far = send(split(found_part), 0, 2).astype(F32)
        rows = [found_part[0] + far[0], found_part[1] + (far[1] + far[2])]
        summed = jnp.concatenate(rows + [weight] * (b > 0), axis=0)
        sums.append((summed, send(summed, 0, 1)))

    steps, grads = [], []
    partner = call(
        partner_kernel,
        (
            like((2, tokens, iheads * tokens), F32),
            like((2, tokens, iheads * index_width), BF16),
        ),
        [vmem()] * 4,
        limit=8 << 20,
        flops=2 * tokens * tokens * iheads * index_width,
        moved=tokens * tokens * iheads * 12,
    )
    for b in range(wide):
        if b:
            both = partner(ikeys[b], found[b][1], iquery, their_iquery)
        else:
            both = (found[b][1][None], iquery[None])
        cores = both[0].shape[0]
        grad_block = call(
            functools.partial(key_grad_kernel, b),
            (
                like((tokens, index_width), BF16),
                like((cores, tokens, iheads * tokens), BF16),
                like((tokens, tokens), F32),
            ),
            [vmem()] * 7,
            limit=8 << 20,
            flops=2 * cores * tokens * tokens * iheads * index_width,
            moved=cores * tokens * tokens * iheads * 6,
        )
        grad, coef, difference = grad_block(live, *sums[b], lse_row, weight, *both)
        steps.append((coef, difference, found[b][1], ikeys[b]))
        grads.append(grad)

    far = send(grads[0], 0, 2)
    own_grad = grads[0].astype(F32) + far.astype(F32)
    others = 0.0
    for b in range(1, wide):
        cross = send(grads[b], b, 2)
        near = send(grads[b], b, 0)
        others = others + (near.astype(F32) + cross.astype(F32))
    own_grad = own_grad + send(own_grad, 0, 1)

    grad_query, grad_weight = call(
        functools.partial(query_grad_kernel, wide),
        (like((tokens, iheads * index_width), F32), like((iheads, tokens), F32)),
        [vmem()] * (4 * wide),
        limit=8 << 20,
        flops=2 * wide * tokens * tokens * iheads * index_width,
        moved=wide * tokens * tokens * iheads * 6,
    )(*(x for kind in zip(*steps) for x in kind))

    return grad_query, grad_weight, own_grad + others


def solution(mesh):
    in_specs = (
        P(("seq", "wide"), "narrow"),
        P(("seq", "wide"), None),
        P("narrow", ("seq", "wide")),
        P(("seq", "wide"), "narrow"),
        P(("seq", "wide"), None),
        P("narrow", ("seq", "wide")),
        P(("seq", "wide")),
        P("seq"),
    )
    out_specs = (
        P(("seq", "wide"), "narrow"),
        P("narrow", ("seq", "wide")),
        P(("seq", "wide"), None),
    )
    return jax.shard_map(
        body,
        mesh=mesh,
        in_specs=in_specs,
        out_specs=out_specs,
        check_vma=False,
    )
```
